512 devices in a mesh: tile: 64 (over y, z), lev: 8 (over x, core).
Axes of the slice: x: 4, y: 8, z: 8, core: 2. Of those that a mesh axis runs over, the one named last changes fastest.
Arguments:
- adjoint: float32 [8, 256, 128, 128], P(None, 'tile', 'lev'), may hold values from -6 to 6
- courant: float32 [3, 256, 128, 128], P(None, 'tile', 'lev'), may hold values from -0.25 to 0.25
- diffusion: float32 [256, 128, 128], P('tile', 'lev'), may hold values from 0.01 to 0.06
- heights: int32 [256, 128], P('tile'), may hold values from 0 to 47, as said below
- dep_coef: float32 [8, 2097152], P(None, ('tile', 'lev')), may hold values from 0.02 to 0.2
- elem_dest: int32 [2097152, 1], P(('tile', 'lev')), may hold values from 0 to 63; in each aligned block of 4096 rows (0 to 4095, 4096 to 8191, ...) at most 128 rows name the same one
- elem_cell: int32 [2097152], P(('tile', 'lev')), may hold values from 0 to 8191
- seg_map: int32 [256, 128], P('tile'), may hold values from 0 to 4095, as said below
- emis_profile: float32 [128], P('lev'), may hold values from 0.004 to 0.04
Outputs:
- adjoint_old: float32 [8, 256, 128, 128], P(None, 'tile', 'lev')
- deposit_sense: float32 [8, 2097152], P(None, ('tile', 'lev'))
- segment_sense: float32 [8, 4096], P(None, ('tile', 'lev'))
The draws below stay inside these ranges and needn't reach their ends.
Inputs may be any that keep to these rules, and one draw needn't show every extreme that they name: `elem_dest`: in the rows of one device at most 128 name the same tile, a bound that some block reaches of them. `heights`: constant over footprints of 4 x 4 columns; 0 in streets. `seg_map`: constant over patches of 4 x 8 columns.
All inputs are finite; a program needn't handle non-finite values.
Results may differ from the reference program's by a relative error of at most 0.00002.
Values sent between devices are 32-bit elements; how exact they have to be, the bound alone decides.
A program may use at most 64 MiB of HBM per device.

```python
import math
import jax
import jax.numpy as jnp
import numpy as np
from jax import lax

TAGS = 8
CX = 4
NY = 128
CZ = 16
CAP = 128
NX = 256
NZ = 128
ELEM_DEV = 4096
ELEMENTS = 2097152
SEGMENTS = 4096
N_TILE = 64
N_LEV = 8


def draw_heights(key, part):
    first_key, second_key = jax.random.split(jax.random.fold_in(key, 11))
    built = jax.random.randint(first_key, (NX // 4, NY // 4), 0, 2)
    tallness = jax.random.randint(second_key, (NX // 4, NY // 4), 2, 3 * CZ)
    footprint = built * tallness
    return jnp.repeat(jnp.repeat(footprint, 4, axis=0), 4, axis=1).astype(jnp.int32)


def draw_seg_map(key, part):
    patches = jax.random.randint(jax.random.fold_in(key, 23), (NX // 4, NY // 8), 0, SEGMENTS)
    return jnp.repeat(jnp.repeat(patches, 4, axis=0), 8, axis=1).astype(jnp.int32)


def set_ends(values, own_key, low, top_value):
    spot = [jax.random.randint(jax.random.fold_in(own_key, axis), (), 0, length) for axis, length in enumerate(values.shape)]
    main_axis = values.shape.index(max(values.shape))
    beside = spot[:main_axis] + [(spot[main_axis] + 1) % values.shape[main_axis]] + spot[main_axis + 1:]
    return values.at[tuple(spot)].set(low).at[tuple(beside)].set(top_value)


def shard_levels(rng, shape, pieces, smallest, top_value):
    def one(dim, shards_of):
        steps = jax.random.uniform(jax.random.fold_in(jax.random.fold_in(rng, 6), dim), (shards_of,), jnp.float32, smallest / len(pieces), top_value / len(pieces))
        return jnp.repeat(jnp.exp(steps), shape[dim] // shards_of).reshape((-1,) + (1,) * (len(shape) - dim - 1))

    level = one(*pieces[0])
    for cut in pieces[1:]:
        level = level * one(*cut)
    return level


def deal_out(own_key, own, number, rows, number_of, top, most, skew):
    order = jax.random.permutation(own_key, number_of)
    packed, common = shares(number_of, rows * top, most, skew, True), shares(number_of, rows * top, most, skew, False)
    places = jnp.arange(number_of)

    def named(sizes, offset_by):
        used = int((sizes > 0).sum())
        fixed = max(1, used // 4)
        shifted = fixed + (places - fixed + offset_by * (used - fixed)) % max(1, number_of - fixed)
        return jnp.zeros((number_of,), jnp.int32).at[order[jnp.where(places < fixed, places, shifted)]].set(jnp.asarray(sizes, jnp.int32))

    sizes = jnp.where(number % 4 == 0, named(packed, number // 4), named(common, number - number // 4 - 1))
    mixed = jax.random.permutation(jax.random.fold_in(own, 3), number_of)
    giver, taker = mixed[0:number_of // 2 * 2:2], mixed[1:number_of // 2 * 2:2]
    slack = jnp.minimum(sizes[giver] - 1, most - sizes[taker]) // 2
    slack = jnp.where((giver == order[0]) | (taker == order[0]) | (sizes[taker] == 0), 0, jnp.maximum(slack, 0))
    shifted = jax.random.randint(jax.random.fold_in(own, 4), (number_of // 2,), 0, 1 << 20) % (slack + 1)
    sizes = sizes.at[giver].add(-shifted).at[taker].add(shifted)
    labels = jnp.searchsorted(jnp.cumsum(sizes), jnp.arange(rows * top), side="right").astype(jnp.int32)
    grid = labels.reshape(top, rows).T
    grid = grid[jax.random.permutation(jax.random.fold_in(own, 1), rows)]
    offset_by = jax.random.randint(jax.random.fold_in(own, 2), (rows, 1), 0, top)
    return jnp.take_along_axis(grid, (jnp.arange(top)[None, :] + offset_by) % top, axis=1)


def shares(number_of, total, bound, lean, full):
    loads = [(1 << 20) // math.isqrt(rank ** lean) + 1 for rank in range(1, number_of + 1)]
    largest = bound if full else min(bound, max(-(-total // number_of), total * loads[0] // sum(loads)))
    least = 1 if total - largest >= number_of - 1 else 0
    given, surplus = [largest] + [least] * (number_of - 1), total - largest - least * (number_of - 1)
    while surplus > 0:
        candidates = [i for i in range(1, number_of) if given[i] < largest] or [i for i in range(1, number_of) if given[i] < bound]
        pool, budget = sum([loads[i] for i in candidates]), surplus
        for i in candidates:
            extra = min(bound - given[i], max(1, budget * loads[i] // pool), surplus)
            given[i] = given[i] + extra
            surplus = surplus - extra
    return np.array(given)


def noise(key, dims, width, bound, cuts=(), held_as=jnp.bfloat16):
    loudness = shard_levels(key, dims, cuts, -0.22, 0.18) if cuts else 1.0
    values = jax.random.normal(key, dims, jnp.float32) * width * loudness
    return jnp.minimum(jnp.maximum(values, -bound), bound).astype(held_as)


def setup_inputs(seed: int = 0) -> dict:
    streams_of = jax.random.split(jax.random.key(seed), 10)
    adjoint = noise(streams_of[0], (TAGS, NX, NZ, NY), 1.0, 6.0, ((1, 64), (2, 8)), jnp.float32)
    courant = jnp.clip(jax.random.uniform(streams_of[1], (3, NX, NZ, NY), jnp.float32, -0.25, 0.25) * shard_levels(streams_of[1], (3, NX, NZ, NY), ((1, 64), (2, 8)), -0.4, 0.0), -0.25, 0.25)
    diffusion = jnp.clip(jnp.exp(math.log(0.06) - 1.7917595 * jax.random.uniform(streams_of[2], (NX, NZ, NY), jnp.float32) ** shard_levels(streams_of[2], (NX, NZ, NY), ((0, 64), (1, 8)), -0.2, 0.2)), 0.01, 0.06)
    heights = draw_heights(jax.random.fold_in(streams_of[9], 71), 0)
    dep_coef = jnp.clip(jnp.exp(math.log(0.2) - 2.3025851 * jax.random.uniform(streams_of[4], (TAGS, ELEMENTS), jnp.float32) ** shard_levels(streams_of[4], (TAGS, ELEMENTS), ((1, 512),), -0.2, 0.2)), 0.02, 0.2)
    elem_dest_keys = jax.random.split(jax.random.fold_in(streams_of[5], 1), ELEMENTS // ELEM_DEV)
    elem_dest_turns = jax.random.permutation(jax.random.fold_in(streams_of[5], 3), ELEMENTS // ELEM_DEV)
    elem_dest = jax.vmap(lambda own, number: deal_out(jax.random.fold_in(streams_of[5], 2), own, number, ELEM_DEV, N_TILE, 1, CAP, 2))(elem_dest_keys, elem_dest_turns).reshape((ELEMENTS, 1))
    elem_cell = set_ends(jax.random.randint(streams_of[6], (ELEMENTS,), 0, CX * CZ * NY), jax.random.fold_in(streams_of[6], 1), 0, (CX * CZ * NY) - 1).astype(jnp.int32)
    seg_map = draw_seg_map(jax.random.fold_in(streams_of[9], 71), 0)
    emis_profile = jnp.clip(jnp.exp(math.log(0.04) - 2.30258502 * jax.random.uniform(streams_of[8], (NZ,), jnp.float32) ** shard_levels(streams_of[8], (NZ,), ((0, 8),), -0.2, 0.2)), 0.004, 0.04)
    return {"adjoint": adjoint, "courant": courant, "diffusion": diffusion, "heights": heights, "dep_coef": dep_coef, "elem_dest": elem_dest, "elem_cell": elem_cell, "seg_map": seg_map, "emis_profile": emis_profile}


def along_y(values, stride):
    zeroes = jnp.zeros_like(values[..., :1])
    if stride > 0:
        return jnp.concatenate([values[..., 1:], zeroes], axis=-1)
    return jnp.concatenate([zeroes, values[..., :-1]], axis=-1)


def interior(values):
    return values[..., 1:-1, 1:-1, :]


def offset_x(values, stride):
    extent = values.shape[-3]
    return values[..., 1 + stride:extent - 1 + stride, 1:-1, :]


def offset_z(values, stride):
    extent = values.shape[-2]
    return values[..., 1:-1, 1 + stride:extent - 1 + stride, :]


def face_terms(centre, forward, backward, diff_c, diff_f, diff_b, wet_c, wet_f, wet_b, cour_c, cour_b):
    open_ahead = wet_c * wet_f
    open_behind = wet_b * wet_c
    cour_ahead = cour_c * open_ahead
    mix_ahead = 0.5 * (diff_c + diff_f) * open_ahead
    cour_behind = cour_b * open_behind
    mix_behind = 0.5 * (diff_b + diff_c) * open_behind
    return (jnp.maximum(cour_ahead, 0.0) + mix_ahead) * (forward - centre) + (jnp.minimum(cour_behind, 0.0) - mix_behind) * (centre - backward)


def apply_adjoint(padded, diff_p, wet_p, cour_xp, cour_zp, cour_yc, deposit):
    centre = interior(padded)
    diff_c = interior(diff_p)
    wet_c = interior(wet_p)
    summed = face_terms(centre, offset_x(padded, 1), offset_x(padded, -1), diff_c, offset_x(diff_p, 1), offset_x(diff_p, -1), wet_c, offset_x(wet_p, 1), offset_x(wet_p, -1), interior(cour_xp), offset_x(cour_xp, -1))
    summed = summed + face_terms(centre, offset_z(padded, 1), offset_z(padded, -1), diff_c, offset_z(diff_p, 1), offset_z(diff_p, -1), wet_c, offset_z(wet_p, 1), offset_z(wet_p, -1), interior(cour_zp), offset_z(cour_zp, -1))
    summed = summed + face_terms(centre, along_y(centre, 1), along_y(centre, -1), diff_c, along_y(diff_c, 1), along_y(diff_c, -1), wet_c, along_y(wet_c, 1), along_y(wet_c, -1), cour_yc, along_y(cour_yc, -1))
    return summed - deposit * centre


def padded_xz(values):
    return jnp.pad(values, ((1, 1), (1, 1), (0, 0)))


def reference(adjoint, courant, diffusion, heights, dep_coef, elem_dest, elem_cell, seg_map, emis_profile):
    levels = jnp.arange(NZ, dtype=jnp.int32)
    wetness = (levels[None, :, None] >= heights[:, None, :]).astype(jnp.float32)
    device = jnp.arange(ELEMENTS, dtype=jnp.int32) // ELEM_DEV
    level_group = device % N_LEV
    dest_tile = elem_dest[:, 0]
    glob_x = dest_tile * CX + elem_cell // (CZ * NY)
    glob_z = level_group * CZ + (elem_cell // NY) % CZ
    glob_y = elem_cell % NY
    flat_cell = ((glob_x * NZ + glob_z) * NY + glob_y).astype(jnp.int32)
    diff_p = padded_xz(diffusion)
    wet_p = padded_xz(wetness)
    cour_xp = padded_xz(courant[0])
    cour_zp = padded_xz(courant[2])
    cour_yc = courant[1]

    def one_tag(inputs):
        tag_field, coef_row = inputs
        deposit = jax.ops.segment_sum(coef_row, flat_cell, num_segments=NX * NZ * NY).reshape(NX, NZ, NY) * wetness
        current = tag_field
        for divisor in (3.0, 2.0, 1.0):
            current = tag_field + apply_adjoint(padded_xz(current), diff_p, wet_p, cour_xp, cour_zp, cour_yc, deposit) / divisor
        return current

    adjoint_old = lax.map(one_tag, (adjoint, dep_coef))
    flat_old = adjoint_old.reshape(TAGS, -1)
    deposit_sense = dep_coef * flat_old[:, flat_cell]
    weights = wetness * emis_profile[None, :, None]
    columns = jnp.sum(adjoint_old * weights[None], axis=2)
    segment_sense = jax.ops.segment_sum(columns.reshape(TAGS, -1).T, seg_map.reshape(-1), num_segments=SEGMENTS).T
    return adjoint_old, deposit_sense, segment_sense
```

```python
import functools

import jax
import jax.numpy as jnp
from jax import lax
from jax.experimental import pallas as pl
from jax.experimental.pallas import tpu as pltpu
from jax.sharding import PartitionSpec as P

MESH = pl.DeviceIdType.MESH
LANES = 128
F32 = jnp.float32
BF16 = jnp.bfloat16
I32 = jnp.int32
HIGHEST = lax.Precision.HIGHEST


def split2(values):
    first = values.astype(BF16)
    return first, (values - first.astype(F32)).astype(BF16)


def iota(shape, dim):
    return lax.broadcasted_iota(I32, shape, dim)


def rows_to(row, count):
    return jnp.broadcast_to(row, (count, row.shape[-1]))


def nt_dot(a, b, precision=None):
    return lax.dot_general(
        a, b, (((1,), (1,)), ((), ())), precision=precision, preferred_element_type=F32
    )


def one_hot_256(row_int):
    local = rows_to(row_int, 16) - iota((16, row_int.shape[-1]), 0)
    local = local.astype(F32).astype(BF16)
    one, zero = jnp.ones((), BF16), jnp.zeros((), BF16)
    return [jnp.where(local == jnp.full((), 16 * j, BF16), one, zero) for j in range(16)]


def step_kernel(
    n_tile,
    n_lev,
    adj,
    cour,
    diff,
    hts,
    coef,
    dest,
    cell,
    seg,
    emis,
    old_out,
    sense_out,
    seg_out,
    state,
    dep,
    weights,
    wet_s,
    zpad,
    fx_r,
    fx_l,
    fz_u,
    fz_d,
    one_d,
    pref,
    pack_a,
    pack_b,
    snd,
    rcv,
    dep_a,
    cell_b,
    cell_hi,
    dest_hi,
    acc,
    look,
    snd2,
    rcv2,
    look2,
    rows,
    s_a2a,
    r_a2a,
    s_back,
    r_back,
    s_flow,
    r_flow,
    s_halo,
    r_halo,
    s_row,
    r_row,
):
    me = lax.axis_index("tile")
    lev = lax.axis_index("lev")
    right, left = lax.rem(me + 1, n_tile), lax.rem(me + n_tile - 1, n_tile)
    above, below = lax.rem(lev + 1, n_lev), lax.rem(lev + n_lev - 1, n_lev)
    tags, elements = coef.shape
    chunks = elements // LANES
    half = n_tile // 2
    depth = 16
    width = 4

    barrier = pltpu.get_barrier_semaphore()

    def greet(k, carry):
        pl.semaphore_signal(
            barrier,
            inc=1,
            device_id=(lax.rem(me + k, n_tile), lev),
            device_id_type=MESH,
        )
        return carry

    lax.fori_loop(1, n_tile, greet, 0)
    for j in range(1, n_lev):
        pl.semaphore_signal(
            barrier, inc=1, device_id=(me, lax.rem(lev + j, n_lev)), device_id_type=MESH
        )

    def reorder(z, carry):
        for x in range(width):
            state[0, x + 1, z + 1] = adj[pl.ds(x * depth + z, tags, stride=width * depth), :]
        return carry

    lax.fori_loop(0, depth, reorder, 0)

    levels = iota((depth, LANES), 0) + lev * depth
    for x in range(width):
        wet_s[x] = (levels >= rows_to(hts[x : x + 1, :], depth)).astype(F32)
    fx_r[0, 0] = wet_s[width - 1]
    fx_r[0, 1] = diff[width - 1]
    fx_r[0, 2] = cour[0, width - 1]
    fx_l[0, 0] = wet_s[0]
    fx_l[0, 1] = diff[0]
    for x in range(width):
        fz_u[0, x : x + 1] = diff[x, depth - 1 : depth, :]
        fz_u[0, width + x : width + x + 1] = cour[2, x, depth - 1 : depth, :]
        fz_d[0, x : x + 1] = diff[x, 0:1, :]
        fz_d[0, width + x : width + x + 1] = cour[2, x, 0:1, :]

    def mark(c, carry):
        k_row = (dest[pl.ds(c, 1), :] - me + n_tile) & (n_tile - 1)
        one_d[pl.ds(pl.multiple_of(c * n_tile, n_tile), n_tile), :] = (
            (rows_to(k_row, n_tile) == iota((n_tile, LANES), 0)).astype(F32).astype(BF16)
        )
        return carry

    lax.fori_loop(0, chunks, mark, 0)
    upper = (iota((LANES, 2 * LANES), 0) < iota((LANES, 2 * LANES), 1)).astype(F32).astype(BF16)
    pref[...] = jnp.dot(one_d[...], upper, preferred_element_type=F32)

    sub_half = iota((16, LANES), 0) // 8

    def place(c, before):
        at = pl.ds(pl.multiple_of(c * LANES, LANES), LANES)
        k_row = (dest[pl.ds(c, 1), :] - me + n_tile) & (n_tile - 1)
        block = pl.ds(pl.multiple_of(c * n_tile, n_tile), n_tile)
        mine = rows_to(k_row, n_tile) == iota((n_tile, LANES), 0)
        place_row = jnp.sum(
            jnp.where(mine, pref[block, 0:LANES] + before, 0.0), axis=0, keepdims=True
        ).astype(I32)
        hi_row = k_row & (half - 1)
        lo_row = (k_row // half) * LANES + place_row
        dest_hi[pl.ds(c, 1), :] = hi_row
        for j, piece in enumerate(one_hot_256(lo_row)):
            pack_b[16 * j : 16 * j + 16, at] = piece
        first, second = split2(coef[:, at])
        first = jnp.concatenate([first, first], axis=0)
        second = jnp.concatenate([second, second], axis=0)
        local = (rows_to(hi_row, 16) - sub_half).astype(F32).astype(BF16)
        zero = jnp.zeros((), BF16)
        for j in range(half // 2):
            chosen = local == jnp.full((), 2 * j, BF16)
            pack_a[16 * j : 16 * j + 16, at] = jnp.where(chosen, first, zero)
            pack_a[half * 8 + 16 * j : half * 8 + 16 * j + 16, at] = jnp.where(
                chosen, second, zero
            )
        id_row = cell[pl.ds(c, 1), :].astype(F32)
        id_all = jnp.where(
            rows_to(hi_row, half) == iota((half, LANES), 0), rows_to(id_row, half), 0.0
        )
        id_first, id_second = split2(id_all)
        pack_a[half * 16 : half * 17, at] = id_first
        pack_a[half * 17 : half * 18, at] = id_second
        return before + pref[block, LANES : 2 * LANES]

    lax.fori_loop(0, chunks, place, jnp.zeros((n_tile, LANES), F32))
    packed = nt_dot(pack_a[...], pack_b[...])
    for k in range(n_tile):
        hi, lo = k % half, (k // half) * LANES
        snd[k, 0:tags, :] = (
            packed[hi * 8 : hi * 8 + 8, lo : lo + LANES]
            + packed[half * 8 + hi * 8 : half * 8 + hi * 8 + 8, lo : lo + LANES]
        )
        snd[k, tags : tags + 1, :] = (
            packed[half * 16 + hi : half * 16 + hi + 1, lo : lo + LANES]
            + packed[half * 17 + hi : half * 17 + hi + 1, lo : lo + LANES]
        )
        snd[k, tags + 1 : tags + 2, :] = seg[0:1, :].astype(F32)

    pl.semaphore_wait(barrier, n_tile - 1 + n_lev - 1)

    def forward(k):
        return pltpu.make_async_remote_copy(
            src_ref=snd.at[k],
            dst_ref=rcv.at[k],
            send_sem=s_a2a.at[k],
            recv_sem=r_a2a.at[k],
            device_id=(lax.rem(me + k, n_tile), lev),
            device_id_type=MESH,
        )

    def back(k):
        return pltpu.make_async_remote_copy(
            src_ref=snd2.at[k],
            dst_ref=rcv2.at[k],
            send_sem=s_back.at[k],
            recv_sem=r_back.at[k],
            device_id=(lax.rem(me + n_tile - k, n_tile), lev),
            device_id_type=MESH,
        )

    def start_forward(k, carry):
        forward(k).start()
        return carry

    lax.fori_loop(1, n_tile, start_forward, 0)
    rcv[0] = snd[0]

    def halos(step):
        return [
            pltpu.make_async_remote_copy(
                src_ref=source,
                dst_ref=target,
                send_sem=s_halo.at[step, i],
                recv_sem=r_halo.at[step, i],
                device_id=device,
                device_id_type=MESH,
            )
            for i, (source, target, device) in enumerate(
                (
                    (
                        state.at[step, width, pl.ds(1, depth)],
                        state.at[step, 0, pl.ds(1, depth)],
                        (right, lev),
                    ),
                    (
                        state.at[step, 1, pl.ds(1, depth)],
                        state.at[step, width + 1, pl.ds(1, depth)],
                        (left, lev),
                    ),
                    (
                        state.at[step, pl.ds(1, width), depth],
                        state.at[step, pl.ds(1, width), 0],
                        (me, above),
                    ),
                    (
                        state.at[step, pl.ds(1, width), 1],
                        state.at[step, pl.ds(1, width), depth + 1],
                        (me, below),
                    ),
                )
            )
        ]

    flows = [
        pltpu.make_async_remote_copy(
            src_ref=ref.at[0],
            dst_ref=ref.at[1],
            send_sem=s_flow.at[i],
            recv_sem=r_flow.at[i],
            device_id=device,
            device_id_type=MESH,
        )
        for i, (ref, device) in enumerate(
            ((fx_r, (right, lev)), (fx_l, (left, lev)), (fz_u, (me, above)), (fz_d, (me, below)))
        )
    ]
    for copy in flows:
        copy.start()
    for copy in halos(0):
        copy.start()

    for copy in flows:
        copy.wait_recv()
    inner_left = (me > 0).astype(F32)
    inner_right = (me < n_tile - 1).astype(F32)
    wet_p = [fx_r[1, 0] * inner_left] + [wet_s[x] for x in range(width)] + [fx_l[1, 0] * inner_right]
    diff_p = [fx_r[1, 1]] + [diff[x] for x in range(width)] + [fx_l[1, 1]]
    cour_p = [fx_r[1, 2]] + [cour[0, x] for x in range(width)]

    def face(wet_a, wet_b, diff_a, diff_b, courant):
        opened = wet_a * wet_b
        a = courant * opened
        k = 0.5 * (diff_a + diff_b) * opened
        return jnp.maximum(a, 0.0) + k, k - jnp.minimum(a, 0.0)

    for f in range(width + 1):
        ahead, behind = face(wet_p[f], wet_p[f + 1], diff_p[f], diff_p[f + 1], cour_p[f])
        if f > 0:
            weights[0, f - 1] = ahead
        if f < width:
            weights[1, f] = behind
    last_lane = iota((depth, LANES), 1) == LANES - 1
    for x in range(width):
        zpad[0, 8 : 8 + depth] = diff[x]
        zpad[0, 7:8] = fz_u[1, x : x + 1]
        zpad[0, 8 + depth : 9 + depth] = fz_d[1, x : x + 1]
        zpad[1, 8 : 8 + depth] = cour[2, x]
        zpad[1, 7:8] = fz_u[1, width + x : width + x + 1]
        height = rows_to(hts[x : x + 1, :], depth)
        wet = wet_s[x]
        wet_up = ((levels + 1 >= height) & (levels + 1 < n_lev * depth)).astype(F32)
        wet_dn = ((levels - 1 >= height) & (levels >= 1)).astype(F32)
        ahead, _ = face(wet, wet_up, diff[x], zpad[0, 9 : 9 + depth], cour[2, x])
        _, behind = face(wet_dn, wet, zpad[0, 7 : 7 + depth], diff[x], zpad[1, 7 : 7 + depth])
        weights[2, x] = ahead
        weights[3, x] = behind
        wet_next = jnp.where(last_lane, 0.0, pltpu.roll(wet, LANES - 1, 1))
        ahead, behind = face(wet, wet_next, diff[x], pltpu.roll(diff[x], LANES - 1, 1), cour[1, x])
        weights[4, x] = ahead
        weights[5, x] = pltpu.roll(behind, 1, 1)

    group = dep_a.shape[1] // LANES
    acc[...] = jnp.zeros_like(acc)

    def gather_group(g, carry):
        for i in range(group):
            k = g * group + i

            @pl.when(k > 0)
            def _():
                forward(k).wait_recv()

            at = pl.ds(pl.multiple_of(k * LANES, LANES), LANES)
            id_row = rcv[k, tags : tags + 1, :].astype(I32)
            hi_row = ((id_row >> 11) & 1) * 16 + ((id_row >> 7) & 15)
            lo_row = (id_row >> 12) * LANES + (id_row & 127)
            cell_hi[pl.ds(k, 1), :] = hi_row
            for j, piece in enumerate(one_hot_256(lo_row)):
                cell_b[16 * j : 16 * j + 16, at] = piece
            first, second = split2(rcv[k, 0:tags, :])
            first = jnp.concatenate([first, first], axis=0)
            second = jnp.concatenate([second, second], axis=0)
            local = (rows_to(hi_row, 16) - sub_half).astype(F32).astype(BF16)
            zero = jnp.zeros((), BF16)
            for j in range(16):
                chosen = local == jnp.full((), 2 * j, BF16)
                dep_a[16 * j : 16 * j + 16, i * LANES : (i + 1) * LANES] = jnp.where(
                    chosen, first, zero
                )
                dep_a[256 + 16 * j : 272 + 16 * j, i * LANES : (i + 1) * LANES] = jnp.where(
                    chosen, second, zero
                )
        span = pl.ds(pl.multiple_of(g * group * LANES, group * LANES), group * LANES)
        acc[...] += nt_dot(dep_a[...], cell_b[:, span])
        return carry

    lax.fori_loop(0, n_tile // group, gather_group, 0)

    def finish_deposit(z, carry):
        for x in range(width):
            row = pl.multiple_of(((x & 1) * depth + z) * 8, 8)
            lo = (x >> 1) * LANES
            total = acc[pl.ds(row, 8), lo : lo + LANES] + acc[pl.ds(row + 256, 8), lo : lo + LANES]
            dep[x, z] = total * rows_to(wet_s[x, pl.ds(z, 1), :], 8)
        return carry

    lax.fori_loop(0, depth, finish_deposit, 0)

    for step, scale in enumerate((1.0 / 3.0, 0.5, 1.0)):
        if step > 0:
            for copy in halos(step):
                copy.start()
        for copy in halos(step):
            copy.wait_recv()

        def stage(z, carry, step=step, scale=scale):
            for x in range(width):

                def weight(d):
                    return rows_to(weights[d, x, pl.ds(z, 1), :], 8)

                centre = state[step, x + 1, z + 1]
                total = weight(0) * (state[step, x + 2, z + 1] - centre)
                total += weight(1) * (state[step, x, z + 1] - centre)
                total += weight(2) * (state[step, x + 1, z + 2] - centre)
                total += weight(3) * (state[step, x + 1, z] - centre)
                total += weight(4) * (pltpu.roll(centre, LANES - 1, 1) - centre)
                total += weight(5) * (pltpu.roll(centre, 1, 1) - centre)
                total -= dep[x, z] * centre
                new = state[0, x + 1, z + 1] + total * scale
                state[step + 1, x + 1, z + 1] = new
                if step == 2:
                    old_out[pl.ds(x * depth + z, tags, stride=width * depth), :] = new
                    carry = carry + new * rows_to(wet_s[x, pl.ds(z, 1), :] * emis[z], 8)
            return carry

        sums = lax.fori_loop(0, depth, stage, jnp.zeros((tags, LANES), F32))

    same_patch = (iota((LANES, LANES), 0) // 8 == iota((LANES, LANES), 1) // 8).astype(F32)
    patch = jnp.dot(sums, same_patch, precision=HIGHEST, preferred_element_type=F32)
    own_lane = iota((tags, LANES), 1) % 8 == iota((tags, LANES), 0)
    own_row = jnp.sum(jnp.where(own_lane, patch, 0.0), axis=0, keepdims=True)
    rows[0] = own_row

    def row_copy(j):
        return pltpu.make_async_remote_copy(
            src_ref=rows.at[0],
            dst_ref=rows.at[j],
            send_sem=s_row.at[j],
            recv_sem=r_row.at[j],
            device_id=(me, lax.rem(lev + j, n_lev)),
            device_id_type=MESH,
        )

    for j in range(1, n_lev):
        row_copy(j).start()

    def table(pair, carry):
        for x in range(width):
            values = jnp.concatenate(
                [state[3, x + 1, 2 * pair + 1], state[3, x + 1, 2 * pair + 2]], axis=0
            )
            first, second = split2(values)
            row = pl.multiple_of(((x & 1) * (depth // 2) + pair) * 16, 16)
            lo = (x >> 1) * LANES
            look[pl.ds(row, 16), lo : lo + LANES] = first
            look[pl.ds(row, 16), 256 + lo : 256 + lo + LANES] = second
        return carry

    lax.fori_loop(0, depth // 2, table, 0)
    total_row = own_row
    for j in range(1, n_lev):
        row_copy(j).wait_recv()
        total_row = total_row + rows[j]

    span_blocks = 4

    def read_group(g, carry):
        at = pl.ds(pl.multiple_of(g * span_blocks * LANES, span_blocks * LANES), span_blocks * LANES)
        hot = cell_b[:, at]
        found = jnp.dot(
            look[...], jnp.concatenate([hot, hot], axis=0), preferred_element_type=F32
        )
        for i in range(span_blocks):
            k = g * span_blocks + i
            hi_all = rows_to(cell_hi[pl.ds(k, 1), :], 8)
            value = jnp.zeros((8, LANES), F32)
            for hi in range(32):
                value += jnp.where(
                    hi_all == hi, found[hi * 8 : hi * 8 + 8, i * LANES : (i + 1) * LANES], 0.0
                )
            snd2[k, 0:tags, :] = value
            snd2[k, tags : tags + 1, :] = total_row

            @pl.when(k > 0)
            def _():
                back(k).start()

        return carry

    lax.fori_loop(0, n_tile // span_blocks, read_group, 0)
    rcv2[0] = snd2[0]

    for j in range(half // 2):
        for d in range(2):
            for i in range(2):
                if d * half + 2 * j + i > 0:
                    back(d * half + 2 * j + i).wait_recv()
            values = jnp.concatenate(
                [rcv2[d * half + 2 * j, 0:tags, :], rcv2[d * half + 2 * j + 1, 0:tags, :]], axis=0
            )
            first, second = split2(values)
            look2[16 * j : 16 * j + 16, d * LANES : (d + 1) * LANES] = first
            look2[16 * j : 16 * j + 16, 256 + d * LANES : 256 + (d + 1) * LANES] = second

    def sense_group(g, carry):
        at = pl.ds(pl.multiple_of(g * span_blocks * LANES, span_blocks * LANES), span_blocks * LANES)
        hot = pack_b[:, at]
        found = jnp.dot(
            look2[...], jnp.concatenate([hot, hot], axis=0), preferred_element_type=F32
        )
        for i in range(span_blocks):
            c = g * span_blocks + i
            one = pl.ds(pl.multiple_of(c * LANES, LANES), LANES)
            hi_all = rows_to(dest_hi[pl.ds(c, 1), :], 8)
            value = jnp.zeros((8, LANES), F32)
            for hi in range(half):
                value += jnp.where(
                    hi_all == hi, found[hi * 8 : hi * 8 + 8, i * LANES : (i + 1) * LANES], 0.0
                )
            sense_out[:, one] = value * coef[:, one]
        return carry

    lax.fori_loop(0, chunks // span_blocks, sense_group, 0)

    first_segment = ((me * n_lev + lev) * 8).astype(F32)
    wanted = iota((8, LANES), 0).astype(F32) + first_segment

    def add_tile(k, total):
        named = rows_to(rcv[lax.rem(n_tile - k, n_tile), tags + 1 : tags + 2, :], 8)
        values = rows_to(rcv2[k, tags : tags + 1, :], 8)
        return total + jnp.where(named == wanted, values, 0.0)

    by_segment = lax.fori_loop(0, n_tile, add_tile, jnp.zeros((8, LANES), F32))
    seg_out[...] = nt_dot(own_lane.astype(F32), by_segment, precision=HIGHEST)

    for copy in flows:
        copy.wait_send()
    for step in range(3):
        for copy in halos(step):
            copy.wait_send()
    for j in range(1, n_lev):
        row_copy(j).wait_send()

    def drain(k, carry):
        forward(k).wait_send()
        back(k).wait_send()
        return carry

    lax.fori_loop(1, n_tile, drain, 0)


def local(
    n_tile, n_lev, adjoint, courant, diffusion, heights, dep_coef, elem_dest, elem_cell, seg_map, emis_profile
):
    tags, width, depth, _ = adjoint.shape
    elements = dep_coef.shape[1]
    half = n_tile // 2
    vmem = pl.BlockSpec(memory_space=pltpu.VMEM)
    smem = pl.BlockSpec(memory_space=pltpu.SMEM)
    dma = pltpu.SemaphoreType.DMA
    group = min(8, n_tile)
    old, sense, segments = pl.pallas_call(
        functools.partial(step_kernel, n_tile, n_lev),
        out_shape=(
            jax.ShapeDtypeStruct((tags * width * depth, LANES), F32),
            jax.ShapeDtypeStruct((tags, elements), F32),
            jax.ShapeDtypeStruct((tags, 8), F32),
        ),
        in_specs=[vmem] * 8 + [smem],
        out_specs=(vmem, vmem, vmem),
        scratch_shapes=[
            pltpu.VMEM((4, width + 2, depth + 2, tags, LANES), F32),
            pltpu.VMEM((width, depth, tags, LANES), F32),
            pltpu.VMEM((6, width, depth, LANES), F32),
            pltpu.VMEM((width, depth, LANES), F32),
            pltpu.VMEM((2, 32, LANES), F32),
            pltpu.VMEM((2, 3, depth, LANES), F32),
            pltpu.VMEM((2, 2, depth, LANES), F32),
            pltpu.VMEM((2, 8, LANES), F32),
            pltpu.VMEM((2, 8, LANES), F32),
            pltpu.VMEM((elements // LANES * n_tile, LANES), BF16),
            pltpu.VMEM((elements // LANES * n_tile, 2 * LANES), F32),
            pltpu.VMEM((half * 18, elements), BF16),
            pltpu.VMEM((256, elements), BF16),
            pltpu.VMEM((n_tile, tags + 2, LANES), F32),
            pltpu.VMEM((n_tile, tags + 2, LANES), F32),
            pltpu.VMEM((512, group * LANES), BF16),
            pltpu.VMEM((256, n_tile * LANES), BF16),
            pltpu.VMEM((n_tile, LANES), I32),
            pltpu.VMEM((elements // LANES, LANES), I32),
            pltpu.VMEM((512, 256), F32),
            pltpu.VMEM((256, 512), BF16),
            pltpu.VMEM((n_tile, tags + 1, LANES), F32),
            pltpu.VMEM((n_tile, tags + 1, LANES), F32),
            pltpu.VMEM((half * 8, 512), BF16),
            pltpu.VMEM((n_lev, 1, LANES), F32),
            dma((n_tile,)),
            dma((n_tile,)),
            dma((n_tile,)),
            dma((n_tile,)),
            dma((4,)),
            dma((4,)),
            dma((3, 4)),
            dma((3, 4)),
            dma((n_lev,)),
            dma((n_lev,)),
        ],
        compiler_params=pltpu.CompilerParams(
            collective_id=0, has_side_effects=True, vmem_limit_bytes=56 << 20
        ),
        name="adjoint_step",
    )(
        adjoint.reshape(tags * width * depth, LANES),
        courant,
        diffusion,
        heights,
        dep_coef,
        elem_dest.reshape(elements // LANES, LANES),
        elem_cell.reshape(elements // LANES, LANES),
        seg_map,
        emis_profile,
    )
    return old.reshape(adjoint.shape), sense, segments


def solution(mesh):
    placed = (
        P(None, "tile", "lev", None),
        P(None, "tile", "lev", None),
        P("tile", "lev", None),
        P("tile", None),
        P(None, ("tile", "lev")),
        P(("tile", "lev"), None),
        P(("tile", "lev")),
        P("tile", None),
        P("lev"),
    )
    return jax.shard_map(
        functools.partial(local, mesh.shape["tile"], mesh.shape["lev"]),
        mesh=mesh,
        in_specs=placed,
        out_specs=(
            P(None, "tile", "lev", None),
            P(None, ("tile", "lev")),
            P(None, ("tile", "lev")),
        ),
        check_vma=False,
    )
```

```python
import functools

import jax
import jax.numpy as jnp
from jax import lax
from jax.experimental import pallas as pl
from jax.experimental.pallas import tpu as pltpu
from jax.sharding import PartitionSpec as P

MESH = pl.DeviceIdType.MESH
LANES = 128
F32 = jnp.float32
BF16 = jnp.bfloat16
I32 = jnp.int32
HIGHEST = lax.Precision.HIGHEST


def split2(values):
    first = values.astype(BF16)
    return first, (values - first.astype(F32)).astype(BF16)


def iota(shape, dim):
    return lax.broadcasted_iota(I32, shape, dim)


def rows_to(row, count):
    return jnp.broadcast_to(row, (count, row.shape[-1]))


def nt_dot(a, b, precision=None):
    return lax.dot_general(
        a, b, (((1,), (1,)), ((), ())), precision=precision, preferred_element_type=F32
    )


def one_hot_256(row_int):
    local = rows_to(row_int, 16) - iota((16, row_int.shape[-1]), 0)
    local = local.astype(F32).astype(BF16)
    one, zero = jnp.ones((), BF16), jnp.zeros((), BF16)
    return [jnp.where(local == jnp.full((), 16 * j, BF16), one, zero) for j in range(16)]


def step_kernel(
    n_tile,
    n_lev,
    adj,
    cour,
    diff,
    hts,
    coef,
    dest,
    cell,
    seg,
    emis,
    old_out,
    sense_out,
    seg_out,
    state,
    dep,
    weights,
    wet_s,
    zpad,
    fx_r,
    fx_l,
    fz_u,
    fz_d,
    one_d,
    pref,
    pack_a,
    pack_b,
    snd,
    rcv,
    dep_a,
    cell_b,
    cell_hi,
    dest_hi,
    acc,
    look,
    snd2,
    rcv2,
    look2,
    segs,
    s_a2a,
    r_a2a,
    s_back,
    r_back,
    s_flow,
    r_flow,
    s_halo,
    r_halo,
    s_row,
    r_row,
):
    me = lax.axis_index("tile")
    lev = lax.axis_index("lev")
    right, left = lax.rem(me + 1, n_tile), lax.rem(me + n_tile - 1, n_tile)
    above, below = lax.rem(lev + 1, n_lev), lax.rem(lev + n_lev - 1, n_lev)
    tags, elements = coef.shape
    chunks = elements // LANES
    half = n_tile // 2
    part = half // 2
    depth = 16
    width = 4

    barrier = pltpu.get_barrier_semaphore()

    def greet(k, carry):
        pl.semaphore_signal(
            barrier,
            inc=1,
            device_id=(lax.rem(me + k, n_tile), lev),
            device_id_type=MESH,
        )
        return carry

    lax.fori_loop(1, n_tile, greet, 0)
    for j in range(1, n_lev):
        pl.semaphore_signal(
            barrier, inc=1, device_id=(me, lax.rem(lev + j, n_lev)), device_id_type=MESH
        )

    def reorder(z, carry):
        for x in range(width):
            state[0, x + 1, z + 1] = adj[pl.ds(x * depth + z, tags, stride=width * depth), :]
        return carry

    lax.fori_loop(0, depth, reorder, 0)

    levels = iota((depth, LANES), 0) + lev * depth
    for x in range(width):
        wet_s[x] = (levels >= rows_to(hts[x : x + 1, :], depth)).astype(F32)
    fx_r[0, 0] = wet_s[width - 1]
    fx_r[0, 1] = diff[width - 1]
    fx_r[0, 2] = cour[0, width - 1]
    fx_l[0, 0] = wet_s[0]
    fx_l[0, 1] = diff[0]
    for x in range(width):
        fz_u[0, x : x + 1] = diff[x, depth - 1 : depth, :]
        fz_u[0, width + x : width + x + 1] = cour[2, x, depth - 1 : depth, :]
        fz_d[0, x : x + 1] = diff[x, 0:1, :]
        fz_d[0, width + x : width + x + 1] = cour[2, x, 0:1, :]

    def mark(c, carry):
        k_row = (dest[pl.ds(c, 1), :] - me + n_tile) & (n_tile - 1)
        one_d[pl.ds(pl.multiple_of(c * n_tile, n_tile), n_tile), :] = (
            (rows_to(k_row, n_tile) == iota((n_tile, LANES), 0)).astype(F32).astype(BF16)
        )
        return carry

    lax.fori_loop(0, chunks, mark, 0)
    upper = (iota((LANES, 2 * LANES), 0) < iota((LANES, 2 * LANES), 1)).astype(F32).astype(BF16)
    pref[...] = jnp.dot(one_d[...], upper, preferred_element_type=F32)

    sub_half = iota((16, LANES), 0) // 8

    def place(c, before):
        at = pl.ds(pl.multiple_of(c * LANES, LANES), LANES)
        k_row = (dest[pl.ds(c, 1), :] - me + n_tile) & (n_tile - 1)
        block = pl.ds(pl.multiple_of(c * n_tile, n_tile), n_tile)
        mine = rows_to(k_row, n_tile) == iota((n_tile, LANES), 0)
        place_row = jnp.sum(
            jnp.where(mine, pref[block, 0:LANES] + before, 0.0), axis=0, keepdims=True
        ).astype(I32)
        hi_row = k_row & (half - 1)
        lo_row = (k_row // half) * LANES + place_row
        dest_hi[pl.ds(c, 1), :] = hi_row
        for j, piece in enumerate(one_hot_256(lo_row)):
            pack_b[16 * j : 16 * j + 16, at] = piece
        first, second = split2(coef[:, at])
        first = jnp.concatenate([first, first], axis=0)
        second = jnp.concatenate([second, second], axis=0)
        local = (rows_to(hi_row, 16) - sub_half).astype(F32).astype(BF16)
        zero = jnp.zeros((), BF16)
        for j in range(half // 2):
            chosen = local == jnp.full((), 2 * j, BF16)
            row = j // (part // 2) * part * 18 + j % (part // 2) * 16
            pack_a[row : row + 16, at] = jnp.where(chosen, first, zero)
            pack_a[row + part * 8 : row + part * 8 + 16, at] = jnp.where(chosen, second, zero)
        id_row = cell[pl.ds(c, 1), :].astype(F32)
        id_all = jnp.where(
            rows_to(hi_row, half) == iota((half, LANES), 0), rows_to(id_row, half), 0.0
        )
        id_first, id_second = split2(id_all)
        for q in range(half // part):
            row, own = q * part * 18 + part * 16, slice(q * part, q * part + part)
            pack_a[row : row + part, at] = id_first[own]
            pack_a[row + part : row + 2 * part, at] = id_second[own]
        return before + pref[block, LANES : 2 * LANES]

    lax.fori_loop(0, chunks, place, jnp.zeros((n_tile, LANES), F32))
    seg_row = seg[0:1, :].astype(F32)

    def forward(k):
        return pltpu.make_async_remote_copy(
            src_ref=snd.at[k],
            dst_ref=rcv.at[k],
            send_sem=s_a2a.at[k],
            recv_sem=r_a2a.at[k],
            device_id=(lax.rem(me + k, n_tile), lev),
            device_id_type=MESH,
        )

    def back(k):
        return pltpu.make_async_remote_copy(
            src_ref=snd2.at[k],
            dst_ref=rcv2.at[k],
            send_sem=s_back.at[k],
            recv_sem=r_back.at[k],
            device_id=(lax.rem(me + n_tile - k, n_tile), lev),
            device_id_type=MESH,
        )

    for q in range(half // part):
        packed = nt_dot(pack_a[q * part * 18 : (q + 1) * part * 18, :], pack_b[...])
        if q == 0:
            pl.semaphore_wait(barrier, n_tile - 1 + n_lev - 1)
        for i in range(part):
            for d in range(2):
                k, lo = d * half + q * part + i, slice(d * LANES, (d + 1) * LANES)
                at_id = part * 16 + i
                snd[k, 0:tags, :] = (
                    packed[i * 8 : i * 8 + 8, lo]
                    + packed[part * 8 + i * 8 : part * 8 + i * 8 + 8, lo]
                )
                snd[k, tags : tags + 1, :] = (
                    packed[at_id : at_id + 1, lo] + packed[at_id + part : at_id + part + 1, lo]
                )
                snd[k, tags + 1 : tags + 2, :] = seg_row
                if k > 0:
                    forward(k).start()
                else:
                    rcv[0] = snd[0]

    def halos(step):
        return [
            pltpu.make_async_remote_copy(
                src_ref=source,
                dst_ref=target,
                send_sem=s_halo.at[step, i],
                recv_sem=r_halo.at[step, i],
                device_id=device,
                device_id_type=MESH,
            )
            for i, (source, target, device) in enumerate(
                (
                    (
                        state.at[step, width, pl.ds(1, depth)],
                        state.at[step, 0, pl.ds(1, depth)],
                        (right, lev),
                    ),
                    (
                        state.at[step, 1, pl.ds(1, depth)],
                        state.at[step, width + 1, pl.ds(1, depth)],
                        (left, lev),
                    ),
                    (
                        state.at[step, pl.ds(1, width), depth],
                        state.at[step, pl.ds(1, width), 0],
                        (me, above),
                    ),
                    (
                        state.at[step, pl.ds(1, width), 1],
                        state.at[step, pl.ds(1, width), depth + 1],
                        (me, below),
                    ),
                )
            )
        ]

    flows = [
        pltpu.make_async_remote_copy(
            src_ref=ref.at[0],
            dst_ref=ref.at[1],
            send_sem=s_flow.at[i],
            recv_sem=r_flow.at[i],
            device_id=device,
            device_id_type=MESH,
        )
        for i, (ref, device) in enumerate(
            ((fx_r, (right, lev)), (fx_l, (left, lev)), (fz_u, (me, above)), (fz_d, (me, below)))
        )
    ]
    for copy in flows:
        copy.start()
    for copy in halos(0):
        copy.start()

    for copy in flows:
        copy.wait_recv()
    inner_left = (me > 0).astype(F32)
    inner_right = (me < n_tile - 1).astype(F32)
    wet_p = [fx_r[1, 0] * inner_left] + [wet_s[x] for x in range(width)] + [fx_l[1, 0] * inner_right]
    diff_p = [fx_r[1, 1]] + [diff[x] for x in range(width)] + [fx_l[1, 1]]
    cour_p = [fx_r[1, 2]] + [cour[0, x] for x in range(width)]

    def face(wet_a, wet_b, diff_a, diff_b, courant):
        opened = wet_a * wet_b
        a = courant * opened
        k = 0.5 * (diff_a + diff_b) * opened
        return jnp.maximum(a, 0.0) + k, k - jnp.minimum(a, 0.0)

    for f in range(width + 1):
        ahead, behind = face(wet_p[f], wet_p[f + 1], diff_p[f], diff_p[f + 1], cour_p[f])
        if f > 0:
            weights[0, f - 1] = ahead
        if f < width:
            weights[1, f] = behind
    last_lane = iota((depth, LANES), 1) == LANES - 1
    for x in range(width):
        zpad[0, 8 : 8 + depth] = diff[x]
        zpad[0, 7:8] = fz_u[1, x : x + 1]
        zpad[0, 8 + depth : 9 + depth] = fz_d[1, x : x + 1]
        zpad[1, 8 : 8 + depth] = cour[2, x]
        zpad[1, 7:8] = fz_u[1, width + x : width + x + 1]
        height = rows_to(hts[x : x + 1, :], depth)
        wet = wet_s[x]
        wet_up = ((levels + 1 >= height) & (levels + 1 < n_lev * depth)).astype(F32)
        wet_dn = ((levels - 1 >= height) & (levels >= 1)).astype(F32)
        ahead, _ = face(wet, wet_up, diff[x], zpad[0, 9 : 9 + depth], cour[2, x])
        _, behind = face(wet_dn, wet, zpad[0, 7 : 7 + depth], diff[x], zpad[1, 7 : 7 + depth])
        weights[2, x] = ahead
        weights[3, x] = behind
        wet_next = jnp.where(last_lane, 0.0, pltpu.roll(wet, LANES - 1, 1))
        ahead, behind = face(wet, wet_next, diff[x], pltpu.roll(diff[x], LANES - 1, 1), cour[1, x])
        weights[4, x] = ahead
        weights[5, x] = pltpu.roll(behind, 1, 1)

    group = dep_a.shape[1] // LANES
    acc[...] = jnp.zeros_like(acc)

    def gather_group(g, carry):
        for i in range(group):
            k = g * group + i

            @pl.when(k > 0)
            def _():
                forward(k).wait_recv()

            at = pl.ds(pl.multiple_of(k * LANES, LANES), LANES)
            id_row = rcv[k, tags : tags + 1, :].astype(I32)
            hi_row = ((id_row >> 11) & 1) * 16 + ((id_row >> 7) & 15)
            lo_row = (id_row >> 12) * LANES + (id_row & 127)
            cell_hi[pl.ds(k, 1), :] = hi_row
            for j, piece in enumerate(one_hot_256(lo_row)):
                cell_b[16 * j : 16 * j + 16, at] = piece
            first, second = split2(rcv[k, 0:tags, :])
            first = jnp.concatenate([first, first], axis=0)
            second = jnp.concatenate([second, second], axis=0)
            local = (rows_to(hi_row, 16) - sub_half).astype(F32).astype(BF16)
            zero = jnp.zeros((), BF16)
            for j in range(16):
                chosen = local == jnp.full((), 2 * j, BF16)
                dep_a[16 * j : 16 * j + 16, i * LANES : (i + 1) * LANES] = jnp.where(
                    chosen, first, zero
                )
                dep_a[256 + 16 * j : 272 + 16 * j, i * LANES : (i + 1) * LANES] = jnp.where(
                    chosen, second, zero
                )
        span = pl.ds(pl.multiple_of(g * group * LANES, group * LANES), group * LANES)
        acc[...] += nt_dot(dep_a[...], cell_b[:, span])
        return carry

    lax.fori_loop(0, n_tile // group, gather_group, 0)

    def finish_deposit(z, carry):
        for x in range(width):
            row = pl.multiple_of(((x & 1) * depth + z) * 8, 8)
            lo = (x >> 1) * LANES
            total = acc[pl.ds(row, 8), lo : lo + LANES] + acc[pl.ds(row + 256, 8), lo : lo + LANES]
            dep[x, z] = total * rows_to(wet_s[x, pl.ds(z, 1), :], 8)
        return carry

    lax.fori_loop(0, depth, finish_deposit, 0)

    cells = [(x, z) for x in range(width) for z in range(depth)]
    edge = [c for c in cells if c[0] in (0, width - 1) or c[1] in (0, depth - 1)]
    inner = [c for c in cells if c not in edge]

    def stage(step, which, sums):
        for x, z in which:

            def weight(d):
                return rows_to(weights[d, x, z : z + 1, :], 8)

            centre = state[step, x + 1, z + 1]
            total = weight(0) * (state[step, x + 2, z + 1] - centre)
            total += weight(1) * (state[step, x, z + 1] - centre)
            total += weight(2) * (state[step, x + 1, z + 2] - centre)
            total += weight(3) * (state[step, x + 1, z] - centre)
            total += weight(4) * (pltpu.roll(centre, LANES - 1, 1) - centre)
            total += weight(5) * (pltpu.roll(centre, 1, 1) - centre)
            total -= dep[x, z] * centre
            new = state[0, x + 1, z + 1] + total * (1.0 / 3.0, 0.5, 1.0)[step]
            state[step + 1, x + 1, z + 1] = new
            if step == 2:
                old_out[pl.ds(x * depth + z, tags, stride=width * depth), :] = new
                sums = sums + new * rows_to(wet_s[x, z : z + 1, :] * emis[z], 8)
        return sums

    def drain(copy):
        def one(k, carry):
            copy(k).wait_send()
            return carry

        lax.fori_loop(1, n_tile, one, 0)

    sums = jnp.zeros((tags, LANES), F32)
    for copy in halos(0):
        copy.wait_recv()
    stage(0, edge, sums)
    for copy in halos(1):
        copy.start()
    stage(0, inner, sums)
    stage(1, inner, sums)
    drain(forward)
    for copy in flows + halos(0):
        copy.wait_send()
    for copy in halos(1):
        copy.wait_recv()
    stage(1, edge, sums)
    for copy in halos(2):
        copy.start()
    sums = stage(2, inner, sums)
    for copy in halos(2):
        copy.wait_recv()
    sums = stage(2, edge, sums)

    same_patch = (iota((LANES, LANES), 0) // 8 == iota((LANES, LANES), 1) // 8).astype(F32)
    patch = jnp.dot(sums, same_patch, precision=HIGHEST, preferred_element_type=F32)
    own_lane = iota((tags, LANES), 1) % 8 == iota((tags, LANES), 0)
    own_row = jnp.sum(jnp.where(own_lane, patch, 0.0), axis=0, keepdims=True)
    def table(pair, carry):
        for x in range(width):
            values = jnp.concatenate(
                [state[3, x + 1, 2 * pair + 1], state[3, x + 1, 2 * pair + 2]], axis=0
            )
            first, second = split2(values)
            row = pl.multiple_of(((x & 1) * (depth // 2) + pair) * 16, 16)
            lo = (x >> 1) * LANES
            look[pl.ds(row, 16), lo : lo + LANES] = first
            look[pl.ds(row, 16), 256 + lo : 256 + lo + LANES] = second
        return carry

    lax.fori_loop(0, depth // 2, table, 0)
    span_blocks = min(8, chunks)

    def read_group(g, carry):
        at = pl.ds(pl.multiple_of(g * span_blocks * LANES, span_blocks * LANES), span_blocks * LANES)
        hot = cell_b[:, at]
        found = jnp.dot(
            look[...], jnp.concatenate([hot, hot], axis=0), preferred_element_type=F32
        )
        for i in range(span_blocks):
            k = g * span_blocks + i
            hi_all = rows_to(cell_hi[pl.ds(k, 1), :], 8)
            value = jnp.zeros((8, LANES), F32)
            for hi in range(32):
                value += jnp.where(
                    hi_all == hi, found[hi * 8 : hi * 8 + 8, i * LANES : (i + 1) * LANES], 0.0
                )
            snd2[k, 0:tags, :] = value
            snd2[k, tags : tags + 1, :] = own_row

            @pl.when(k > 0)
            def _():
                back(k).start()

        return carry

    lax.fori_loop(0, n_tile // span_blocks, read_group, 0)
    rcv2[0] = snd2[0]

    for j in range(half // 2):
        for d in range(2):
            for i in range(2):
                if d * half + 2 * j + i > 0:
                    back(d * half + 2 * j + i).wait_recv()
            values = jnp.concatenate(
                [rcv2[d * half + 2 * j, 0:tags, :], rcv2[d * half + 2 * j + 1, 0:tags, :]], axis=0
            )
            first, second = split2(values)
            look2[16 * j : 16 * j + 16, d * LANES : (d + 1) * LANES] = first
            look2[16 * j : 16 * j + 16, 256 + d * LANES : 256 + (d + 1) * LANES] = second

    def wanted(j):
        first_segment = (me * n_lev + lax.rem(lev + j, n_lev)) * 8
        return (iota((8, LANES), 0) + first_segment).astype(F32)

    def segment_copy(j):
        return pltpu.make_async_remote_copy(
            src_ref=segs.at[0, j],
            dst_ref=segs.at[1, j],
            send_sem=s_row.at[j],
            recv_sem=r_row.at[j],
            device_id=(me, lax.rem(lev + j, n_lev)),
            device_id_type=MESH,
        )

    wanted_all = [wanted(j) for j in range(n_lev)]

    def add_tile(k, totals):
        named = rows_to(rcv[lax.rem(n_tile - k, n_tile), tags + 1 : tags + 2, :], 8)
        values = rows_to(rcv2[k, tags : tags + 1, :], 8)
        return tuple(
            total + jnp.where(named == want, values, 0.0)
            for total, want in zip(totals, wanted_all)
        )

    by_segment = lax.fori_loop(
        0, n_tile, add_tile, (jnp.zeros((8, LANES), F32),) * n_lev, unroll=4
    )
    for j in range(1, n_lev):
        segs[0, j] = by_segment[j]
        segment_copy(j).start()

    def sense_group(g, carry):
        at = pl.ds(pl.multiple_of(g * span_blocks * LANES, span_blocks * LANES), span_blocks * LANES)
        hot = pack_b[:, at]
        found = jnp.dot(
            look2[...], jnp.concatenate([hot, hot], axis=0), preferred_element_type=F32
        )
        for i in range(span_blocks):
            c = g * span_blocks + i
            one = pl.ds(pl.multiple_of(c * LANES, LANES), LANES)
            hi_all = rows_to(dest_hi[pl.ds(c, 1), :], 8)
            value = jnp.zeros((8, LANES), F32)
            for hi in range(half):
                value += jnp.where(
                    hi_all == hi, found[hi * 8 : hi * 8 + 8, i * LANES : (i + 1) * LANES], 0.0
                )
            sense_out[:, one] = value * coef[:, one]
        return carry

    lax.fori_loop(0, chunks // span_blocks, sense_group, 0)

    drain(back)
    for copy in halos(1) + halos(2):
        copy.wait_send()

    total = by_segment[0]
    for j in range(1, n_lev):
        segment_copy(j).wait()
        total = total + segs[1, j]
    seg_out[...] = nt_dot(own_lane.astype(F32), total, precision=HIGHEST)


def local(
    n_tile, n_lev, adjoint, courant, diffusion, heights, dep_coef, elem_dest, elem_cell, seg_map, emis_profile
):
    tags, width, depth, _ = adjoint.shape
    elements = dep_coef.shape[1]
    half = n_tile // 2
    vmem = pl.BlockSpec(memory_space=pltpu.VMEM)
    smem = pl.BlockSpec(memory_space=pltpu.SMEM)
    dma = pltpu.SemaphoreType.DMA
    group = min(16, n_tile)
    old, sense, segments = pl.pallas_call(
        functools.partial(step_kernel, n_tile, n_lev),
        out_shape=(
            jax.ShapeDtypeStruct((tags * width * depth, LANES), F32),
            jax.ShapeDtypeStruct((tags, elements), F32),
            jax.ShapeDtypeStruct((tags, 8), F32),
        ),
        in_specs=[vmem] * 8 + [smem],
        out_specs=(vmem, vmem, vmem),
        scratch_shapes=[
            pltpu.VMEM((4, width + 2, depth + 2, tags, LANES), F32),
            pltpu.VMEM((width, depth, tags, LANES), F32),
            pltpu.VMEM((6, width, depth, LANES), F32),
            pltpu.VMEM((width, depth, LANES), F32),
            pltpu.VMEM((2, 32, LANES), F32),
            pltpu.VMEM((2, 3, depth, LANES), F32),
            pltpu.VMEM((2, 2, depth, LANES), F32),
            pltpu.VMEM((2, 8, LANES), F32),
            pltpu.VMEM((2, 8, LANES), F32),
            pltpu.VMEM((elements // LANES * n_tile, LANES), BF16),
            pltpu.VMEM((elements // LANES * n_tile, 2 * LANES), F32),
            pltpu.VMEM((half * 18, elements), BF16),
            pltpu.VMEM((256, elements), BF16),
            pltpu.VMEM((n_tile, tags + 2, LANES), F32),
            pltpu.VMEM((n_tile, tags + 2, LANES), F32),
            pltpu.VMEM((512, group * LANES), BF16),
            pltpu.VMEM((256, n_tile * LANES), BF16),
            pltpu.VMEM((n_tile, LANES), I32),
            pltpu.VMEM((elements // LANES, LANES), I32),
            pltpu.VMEM((512, 256), F32),
            pltpu.VMEM((256, 512), BF16),
            pltpu.VMEM((n_tile, tags + 1, LANES), F32),
            pltpu.VMEM((n_tile, tags + 1, LANES), F32),
            pltpu.VMEM((half * 8, 512), BF16),
            pltpu.VMEM((2, n_lev, 8, LANES), F32),
            dma((n_tile,)),
            dma((n_tile,)),
            dma((n_tile,)),
            dma((n_tile,)),
            dma((4,)),
            dma((4,)),
            dma((3, 4)),
            dma((3, 4)),
            dma((n_lev,)),
            dma((n_lev,)),
        ],
        compiler_params=pltpu.CompilerParams(
            collective_id=0, has_side_effects=True, vmem_limit_bytes=56 << 20
        ),
        name="adjoint_step",
    )(
        adjoint.reshape(tags * width * depth, LANES),
        courant,
        diffusion,
        heights,
        dep_coef,
        elem_dest.reshape(elements // LANES, LANES),
        elem_cell.reshape(elements // LANES, LANES),
        seg_map,
        emis_profile,
    )
    return old.reshape(adjoint.shape), sense, segments


def solution(mesh):
    placed = (
        P(None, "tile", "lev", None),
        P(None, "tile", "lev", None),
        P("tile", "lev", None),
        P("tile", None),
        P(None, ("tile", "lev")),
        P(("tile", "lev"), None),
        P(("tile", "lev")),
        P("tile", None),
        P("lev"),
    )
    return jax.shard_map(
        functools.partial(local, mesh.shape["tile"], mesh.shape["lev"]),
        mesh=mesh,
        in_specs=placed,
        out_specs=(
            P(None, "tile", "lev", None),
            P(None, ("tile", "lev")),
            P(None, ("tile", "lev")),
        ),
        check_vma=False,
    )
```

```python
import functools

import jax
import jax.numpy as jnp
from jax import lax
from jax.experimental import pallas as pl
from jax.experimental.pallas import tpu as pltpu
from jax.sharding import PartitionSpec as P

MESH = pl.DeviceIdType.MESH
LANES = 128
F32 = jnp.float32
BF16 = jnp.bfloat16
I32 = jnp.int32
HIGHEST = lax.Precision.HIGHEST


def split2(values):
    first = values.astype(BF16)
    return first, (values - first.astype(F32)).astype(BF16)


def iota(shape, dim):
    return lax.broadcasted_iota(I32, shape, dim)


def rows_to(row, count):
    return jnp.broadcast_to(row, (count, row.shape[-1]))


def nt_dot(a, b, precision=None):
    return lax.dot_general(
        a, b, (((1,), (1,)), ((), ())), precision=precision, preferred_element_type=F32
    )


def one_hot_256(row_int):
    local = rows_to(row_int, 16) - iota((16, row_int.shape[-1]), 0)
    local = local.astype(F32).astype(BF16)
    one, zero = jnp.ones((), BF16), jnp.zeros((), BF16)
    return [jnp.where(local == jnp.full((), 16 * j, BF16), one, zero) for j in range(16)]


def step_kernel(
    n_tile,
    n_lev,
    adj,
    cour,
    diff,
    hts,
    coef,
    dest,
    cell,
    seg,
    emis,
    old_out,
    sense_out,
    seg_out,
    state,
    dep,
    weights,
    wet_s,
    zpad,
    fx_r,
    fx_l,
    fz_u,
    fz_d,
    one_d,
    pref,
    pack_a,
    pack_b,
    snd,
    rcv,
    dep_a,
    cell_b,
    cell_hi,
    dest_hi,
    acc,
    look,
    snd2,
    rcv2,
    look2,
    segs,
    s_a2a,
    r_a2a,
    s_back,
    r_back,
    s_flow,
    r_flow,
    s_halo,
    r_halo,
    s_row,
    r_row,
    second_round,
):
    me = lax.axis_index("tile")
    lev = lax.axis_index("lev")
    right, left = lax.rem(me + 1, n_tile), lax.rem(me + n_tile - 1, n_tile)
    above, below = lax.rem(lev + 1, n_lev), lax.rem(lev + n_lev - 1, n_lev)
    tags, elements = coef.shape
    chunks = elements // LANES
    half = n_tile // 2
    part = half // 2
    depth = 16
    width = 4

    count_z = min(8, n_tile)
    count_y = n_tile // count_z
    my_y, my_z = me // count_z, lax.rem(me, count_z)
    barrier = pltpu.get_barrier_semaphore()

    def signal(semaphore, tile, level):
        pl.semaphore_signal(semaphore, inc=1, device_id=(tile, level), device_id_type=MESH)

    for j in range(1, count_z):
        signal(barrier, my_y * count_z + lax.rem(my_z + j, count_z), lev)
    for j in range(1, count_y):
        signal(barrier, lax.rem(my_y + j, count_y) * count_z + my_z, lev)
    for j in range(1, n_lev):
        signal(barrier, me, lax.rem(lev + j, n_lev))

    def reorder(z, carry):
        for x in range(width):
            state[0, x + 1, z + 1] = adj[pl.ds(x * depth + z, tags, stride=width * depth), :]
        return carry

    lax.fori_loop(0, depth, reorder, 0)

    levels = iota((depth, LANES), 0) + lev * depth
    for x in range(width):
        wet_s[x] = (levels >= rows_to(hts[x : x + 1, :], depth)).astype(F32)
    fx_r[0, 0] = wet_s[width - 1]
    fx_r[0, 1] = diff[width - 1]
    fx_r[0, 2] = cour[0, width - 1]
    fx_l[0, 0] = wet_s[0]
    fx_l[0, 1] = diff[0]
    for x in range(width):
        fz_u[0, x : x + 1] = diff[x, depth - 1 : depth, :]
        fz_u[0, width + x : width + x + 1] = cour[2, x, depth - 1 : depth, :]
        fz_d[0, x : x + 1] = diff[x, 0:1, :]
        fz_d[0, width + x : width + x + 1] = cour[2, x, 0:1, :]

    def mark(c, carry):
        k_row = (dest[pl.ds(c, 1), :] - me + n_tile) & (n_tile - 1)
        one_d[pl.ds(pl.multiple_of(c * n_tile, n_tile), n_tile), :] = (
            (rows_to(k_row, n_tile) == iota((n_tile, LANES), 0)).astype(F32).astype(BF16)
        )
        return carry

    lax.fori_loop(0, chunks, mark, 0)
    upper = (iota((LANES, 2 * LANES), 0) < iota((LANES, 2 * LANES), 1)).astype(F32).astype(BF16)
    pref[...] = jnp.dot(one_d[...], upper, preferred_element_type=F32)

    sub_half = iota((16, LANES), 0) // 8

    def place(c, before):
        at = pl.ds(pl.multiple_of(c * LANES, LANES), LANES)
        k_row = (dest[pl.ds(c, 1), :] - me + n_tile) & (n_tile - 1)
        block = pl.ds(pl.multiple_of(c * n_tile, n_tile), n_tile)
        mine = rows_to(k_row, n_tile) == iota((n_tile, LANES), 0)
        place_row = jnp.sum(
            jnp.where(mine, pref[block, 0:LANES] + before, 0.0), axis=0, keepdims=True
        ).astype(I32)
        hi_row = k_row & (half - 1)
        lo_row = (k_row // half) * LANES + place_row
        dest_hi[pl.ds(c, 1), :] = hi_row
        for j, piece in enumerate(one_hot_256(lo_row)):
            pack_b[16 * j : 16 * j + 16, at] = piece
        first, second = split2(coef[:, at])
        first = jnp.concatenate([first, first], axis=0)
        second = jnp.concatenate([second, second], axis=0)
        local = (rows_to(hi_row, 16) - sub_half).astype(F32).astype(BF16)
        zero = jnp.zeros((), BF16)
        for j in range(half // 2):
            chosen = local == jnp.full((), 2 * j, BF16)
            row = j // (part // 2) * part * 18 + j % (part // 2) * 16
            pack_a[row : row + 16, at] = jnp.where(chosen, first, zero)
            pack_a[row + part * 8 : row + part * 8 + 16, at] = jnp.where(chosen, second, zero)
        id_row = cell[pl.ds(c, 1), :].astype(F32)
        id_all = jnp.where(
            rows_to(hi_row, half) == iota((half, LANES), 0), rows_to(id_row, half), 0.0
        )
        id_first, id_second = split2(id_all)
        for q in range(half // part):
            row, own = q * part * 18 + part * 16, slice(q * part, q * part + part)
            pack_a[row : row + part, at] = id_first[own]
            pack_a[row + part : row + 2 * part, at] = id_second[own]
        return before + pref[block, LANES : 2 * LANES]

    lax.fori_loop(0, chunks, place, jnp.zeros((n_tile, LANES), F32))
    pl.semaphore_wait(barrier, count_z - 1 + count_y - 1 + n_lev - 1)
    for j in range(1, count_y):
        signal(second_round, lax.rem(my_y + j, count_y) * count_z + my_z, lev)

    seg_row = seg[0:1, :].astype(F32)

    def forward(k):
        return pltpu.make_async_remote_copy(
            src_ref=snd.at[k],
            dst_ref=rcv.at[k],
            send_sem=s_a2a,
            recv_sem=r_a2a.at[k],
            device_id=(lax.rem(me + k, n_tile), lev),
            device_id_type=MESH,
        )

    def back(k):
        return pltpu.make_async_remote_copy(
            src_ref=snd2.at[k],
            dst_ref=rcv2.at[k],
            send_sem=s_back,
            recv_sem=r_back.at[k],
            device_id=(lax.rem(me + n_tile - k, n_tile), lev),
            device_id_type=MESH,
        )

    for q in range(half // part):
        packed = nt_dot(pack_a[q * part * 18 : (q + 1) * part * 18, :], pack_b[...])
        if q == 0 and count_y > 1:
            pl.semaphore_wait(second_round, count_y - 1)
        for i in range(part):
            for d in range(2):
                k, lo = d * half + q * part + i, slice(d * LANES, (d + 1) * LANES)
                at_id = part * 16 + i
                snd[k, 0:tags, :] = (
                    packed[i * 8 : i * 8 + 8, lo]
                    + packed[part * 8 + i * 8 : part * 8 + i * 8 + 8, lo]
                )
                snd[k, tags : tags + 1, :] = (
                    packed[at_id : at_id + 1, lo] + packed[at_id + part : at_id + part + 1, lo]
                )
                snd[k, tags + 1 : tags + 2, :] = seg_row
                if k > 0:
                    forward(k).start()
                else:
                    rcv[0] = snd[0]

    def halos(step):
        return [
            pltpu.make_async_remote_copy(
                src_ref=source,
                dst_ref=target,
                send_sem=s_halo.at[step, i],
                recv_sem=r_halo.at[step, i],
                device_id=device,
                device_id_type=MESH,
            )
            for i, (source, target, device) in enumerate(
                (
                    (
                        state.at[step, width, pl.ds(1, depth)],
                        state.at[step, 0, pl.ds(1, depth)],
                        (right, lev),
                    ),
                    (
                        state.at[step, 1, pl.ds(1, depth)],
                        state.at[step, width + 1, pl.ds(1, depth)],
                        (left, lev),
                    ),
                    (
                        state.at[step, pl.ds(1, width), depth],
                        state.at[step, pl.ds(1, width), 0],
                        (me, above),
                    ),
                    (
                        state.at[step, pl.ds(1, width), 1],
                        state.at[step, pl.ds(1, width), depth + 1],
                        (me, below),
                    ),
                )
            )
        ]

    flows = [
        pltpu.make_async_remote_copy(
            src_ref=ref.at[0],
            dst_ref=ref.at[1],
            send_sem=s_flow.at[i],
            recv_sem=r_flow.at[i],
            device_id=device,
            device_id_type=MESH,
        )
        for i, (ref, device) in enumerate(
            ((fx_r, (right, lev)), (fx_l, (left, lev)), (fz_u, (me, above)), (fz_d, (me, below)))
        )
    ]
    for copy in flows:
        copy.start()
    for copy in halos(0):
        copy.start()

    for copy in flows:
        copy.wait_recv()
    inner_left = (me > 0).astype(F32)
    inner_right = (me < n_tile - 1).astype(F32)
    wet_p = [fx_r[1, 0] * inner_left] + [wet_s[x] for x in range(width)] + [fx_l[1, 0] * inner_right]
    diff_p = [fx_r[1, 1]] + [diff[x] for x in range(width)] + [fx_l[1, 1]]
    cour_p = [fx_r[1, 2]] + [cour[0, x] for x in range(width)]

    def face(wet_a, wet_b, diff_a, diff_b, courant):
        opened = wet_a * wet_b
        a = courant * opened
        k = 0.5 * (diff_a + diff_b) * opened
        return jnp.maximum(a, 0.0) + k, k - jnp.minimum(a, 0.0)

    for f in range(width + 1):
        ahead, behind = face(wet_p[f], wet_p[f + 1], diff_p[f], diff_p[f + 1], cour_p[f])
        if f > 0:
            weights[0, f - 1] = ahead
        if f < width:
            weights[1, f] = behind
    last_lane = iota((depth, LANES), 1) == LANES - 1
    for x in range(width):
        zpad[0, 8 : 8 + depth] = diff[x]
        zpad[0, 7:8] = fz_u[1, x : x + 1]
        zpad[0, 8 + depth : 9 + depth] = fz_d[1, x : x + 1]
        zpad[1, 8 : 8 + depth] = cour[2, x]
        zpad[1, 7:8] = fz_u[1, width + x : width + x + 1]
        height = rows_to(hts[x : x + 1, :], depth)
        wet = wet_s[x]
        wet_up = ((levels + 1 >= height) & (levels + 1 < n_lev * depth)).astype(F32)
        wet_dn = ((levels - 1 >= height) & (levels >= 1)).astype(F32)
        ahead, _ = face(wet, wet_up, diff[x], zpad[0, 9 : 9 + depth], cour[2, x])
        _, behind = face(wet_dn, wet, zpad[0, 7 : 7 + depth], diff[x], zpad[1, 7 : 7 + depth])
        weights[2, x] = ahead
        weights[3, x] = behind
        wet_next = jnp.where(last_lane, 0.0, pltpu.roll(wet, LANES - 1, 1))
        ahead, behind = face(wet, wet_next, diff[x], pltpu.roll(diff[x], LANES - 1, 1), cour[1, x])
        weights[4, x] = ahead
        weights[5, x] = pltpu.roll(behind, 1, 1)

    def slot(place_at):
        source = lax.rem(place_at, count_y) * count_z + place_at // count_y
        return lax.rem(me - source + n_tile, n_tile)

    group = dep_a.shape[1] // LANES
    acc[...] = jnp.zeros_like(acc)

    def gather_group(g, carry):
        for i in range(group):
            place_at = g * group + i
            k = slot(place_at)

            @pl.when(k > 0)
            def _():
                forward(k).wait_recv()

            at = pl.ds(pl.multiple_of(place_at * LANES, LANES), LANES)
            id_row = rcv[k, tags : tags + 1, :].astype(I32)
            hi_row = ((id_row >> 11) & 1) * 16 + ((id_row >> 7) & 15)
            lo_row = (id_row >> 12) * LANES + (id_row & 127)
            cell_hi[pl.ds(place_at, 1), :] = hi_row
            for j, piece in enumerate(one_hot_256(lo_row)):
                cell_b[16 * j : 16 * j + 16, at] = piece
            first, second = split2(rcv[k, 0:tags, :])
            first = jnp.concatenate([first, first], axis=0)
            second = jnp.concatenate([second, second], axis=0)
            local = (rows_to(hi_row, 16) - sub_half).astype(F32).astype(BF16)
            zero = jnp.zeros((), BF16)
            for j in range(16):
                chosen = local == jnp.full((), 2 * j, BF16)
                dep_a[16 * j : 16 * j + 16, i * LANES : (i + 1) * LANES] = jnp.where(
                    chosen, first, zero
                )
                dep_a[256 + 16 * j : 272 + 16 * j, i * LANES : (i + 1) * LANES] = jnp.where(
                    chosen, second, zero
                )
        span = pl.ds(pl.multiple_of(g * group * LANES, group * LANES), group * LANES)
        acc[...] += nt_dot(dep_a[...], cell_b[:, span])
        return carry

    lax.fori_loop(0, n_tile // group, gather_group, 0)

    def finish_deposit(z, carry):
        for x in range(width):
            row = pl.multiple_of(((x & 1) * depth + z) * 8, 8)
            lo = (x >> 1) * LANES
            total = acc[pl.ds(row, 8), lo : lo + LANES] + acc[pl.ds(row + 256, 8), lo : lo + LANES]
            dep[x, z] = total * rows_to(wet_s[x, pl.ds(z, 1), :], 8)
        return carry

    lax.fori_loop(0, depth, finish_deposit, 0)

    cells = [(x, z) for x in range(width) for z in range(depth)]
    edge = [c for c in cells if c[0] in (0, width - 1) or c[1] in (0, depth - 1)]
    inner = [c for c in cells if c not in edge]

    def stage(step, which, sums):
        for x, z in which:

            def weight(d):
                return rows_to(weights[d, x, z : z + 1, :], 8)

            centre = state[step, x + 1, z + 1]
            total = weight(0) * (state[step, x + 2, z + 1] - centre)
            total += weight(1) * (state[step, x, z + 1] - centre)
            total += weight(2) * (state[step, x + 1, z + 2] - centre)
            total += weight(3) * (state[step, x + 1, z] - centre)
            total += weight(4) * (pltpu.roll(centre, LANES - 1, 1) - centre)
            total += weight(5) * (pltpu.roll(centre, 1, 1) - centre)
            total -= dep[x, z] * centre
            new = state[0, x + 1, z + 1] + total * (1.0 / 3.0, 0.5, 1.0)[step]
            state[step + 1, x + 1, z + 1] = new
            if step == 2:
                old_out[pl.ds(x * depth + z, tags, stride=width * depth), :] = new
                sums = sums + new * rows_to(wet_s[x, z : z + 1, :] * emis[z], 8)
        return sums

    def drain(source, target, semaphore):
        pltpu.make_async_remote_copy(
            src_ref=source.at[pl.ds(1, n_tile - 1)],
            dst_ref=target.at[pl.ds(1, n_tile - 1)],
            send_sem=semaphore,
            recv_sem=semaphore,
            device_id=(right, lev),
            device_id_type=MESH,
        ).wait_send()

    sums = jnp.zeros((tags, LANES), F32)
    for copy in halos(0):
        copy.wait_recv()
    stage(0, edge, sums)
    for copy in halos(1):
        copy.start()
    stage(0, inner, sums)
    stage(1, inner, sums)
    drain(snd, rcv, s_a2a)
    for copy in flows + halos(0):
        copy.wait_send()
    for copy in halos(1):
        copy.wait_recv()
    stage(1, edge, sums)
    for copy in halos(2):
        copy.start()
    sums = stage(2, inner, sums)
    for copy in halos(2):
        copy.wait_recv()
    sums = stage(2, edge, sums)

    same_patch = (iota((LANES, LANES), 0) // 8 == iota((LANES, LANES), 1) // 8).astype(F32)
    patch = jnp.dot(sums, same_patch, precision=HIGHEST, preferred_element_type=F32)
    own_lane = iota((tags, LANES), 1) % 8 == iota((tags, LANES), 0)
    own_row = jnp.sum(jnp.where(own_lane, patch, 0.0), axis=0, keepdims=True)
    def table(pair, carry):
        for x in range(width):
            values = jnp.concatenate(
                [state[3, x + 1, 2 * pair + 1], state[3, x + 1, 2 * pair + 2]], axis=0
            )
            first, second = split2(values)
            row = pl.multiple_of(((x & 1) * (depth // 2) + pair) * 16, 16)
            lo = (x >> 1) * LANES
            look[pl.ds(row, 16), lo : lo + LANES] = first
            look[pl.ds(row, 16), 256 + lo : 256 + lo + LANES] = second
        return carry

    lax.fori_loop(0, depth // 2, table, 0)
    span_blocks = min(8, chunks)

    def read_group(g, carry):
        at = pl.ds(pl.multiple_of(g * span_blocks * LANES, span_blocks * LANES), span_blocks * LANES)
        hot = cell_b[:, at]
        found = jnp.dot(
            look[...], jnp.concatenate([hot, hot], axis=0), preferred_element_type=F32
        )
        for i in range(span_blocks):
            place_at = g * span_blocks + i
            k = slot(place_at)
            hi_all = rows_to(cell_hi[pl.ds(place_at, 1), :], 8)
            value = jnp.zeros((8, LANES), F32)
            for hi in range(32):
                value += jnp.where(
                    hi_all == hi, found[hi * 8 : hi * 8 + 8, i * LANES : (i + 1) * LANES], 0.0
                )
            snd2[k, 0:tags, :] = value
            snd2[k, tags : tags + 1, :] = own_row

            @pl.when(k > 0)
            def _():
                back(k).start()

        return carry

    lax.fori_loop(0, n_tile // span_blocks, read_group, 0)
    rcv2[0] = snd2[0]

    def arrive(k, carry):
        back(k).wait_recv()
        return carry

    lax.fori_loop(1, n_tile, arrive, 0)

    def wanted(j):
        first_segment = (me * n_lev + lax.rem(lev + j, n_lev)) * 8
        return (iota((8, LANES), 0) + first_segment).astype(F32)

    def segment_copy(j):
        return pltpu.make_async_remote_copy(
            src_ref=segs.at[0, j],
            dst_ref=segs.at[1, j],
            send_sem=s_row.at[j],
            recv_sem=r_row.at[j],
            device_id=(me, lax.rem(lev + j, n_lev)),
            device_id_type=MESH,
        )

    wanted_all = [wanted(j) for j in range(n_lev)]

    def add_tile(k, totals):
        named = rows_to(rcv[lax.rem(n_tile - k, n_tile), tags + 1 : tags + 2, :], 8)
        values = rows_to(rcv2[k, tags : tags + 1, :], 8)
        return tuple(
            total + jnp.where(named == want, values, 0.0)
            for total, want in zip(totals, wanted_all)
        )

    by_segment = lax.fori_loop(
        0, n_tile, add_tile, (jnp.zeros((8, LANES), F32),) * n_lev, unroll=4
    )
    for j in range(1, n_lev):
        segs[0, j] = by_segment[j]
        segment_copy(j).start()

    for j in range(half // 2):
        for d in range(2):
            values = jnp.concatenate(
                [rcv2[d * half + 2 * j, 0:tags, :], rcv2[d * half + 2 * j + 1, 0:tags, :]], axis=0
            )
            first, second = split2(values)
            look2[16 * j : 16 * j + 16, d * LANES : (d + 1) * LANES] = first
            look2[16 * j : 16 * j + 16, 256 + d * LANES : 256 + (d + 1) * LANES] = second

    def sense_group(g, carry):
        at = pl.ds(pl.multiple_of(g * span_blocks * LANES, span_blocks * LANES), span_blocks * LANES)
        hot = pack_b[:, at]
        found = jnp.dot(
            look2[...], jnp.concatenate([hot, hot], axis=0), preferred_element_type=F32
        )
        for i in range(span_blocks):
            c = g * span_blocks + i
            one = pl.ds(pl.multiple_of(c * LANES, LANES), LANES)
            hi_all = rows_to(dest_hi[pl.ds(c, 1), :], 8)
            value = jnp.zeros((8, LANES), F32)
            for hi in range(half):
                value += jnp.where(
                    hi_all == hi, found[hi * 8 : hi * 8 + 8, i * LANES : (i + 1) * LANES], 0.0
                )
            sense_out[:, one] = value * coef[:, one]
        return carry

    lax.fori_loop(0, chunks // span_blocks, sense_group, 0)

    drain(snd2, rcv2, s_back)
    for copy in halos(1) + halos(2):
        copy.wait_send()

    total = by_segment[0]
    for j in range(1, n_lev):
        segment_copy(j).wait()
        total = total + segs[1, j]
    seg_out[...] = nt_dot(own_lane.astype(F32), total, precision=HIGHEST)


def local(
    n_tile, n_lev, adjoint, courant, diffusion, heights, dep_coef, elem_dest, elem_cell, seg_map, emis_profile
):
    tags, width, depth, _ = adjoint.shape
    elements = dep_coef.shape[1]
    half = n_tile // 2
    vmem = pl.BlockSpec(memory_space=pltpu.VMEM)
    smem = pl.BlockSpec(memory_space=pltpu.SMEM)
    dma = pltpu.SemaphoreType.DMA
    group = min(16, n_tile)
    old, sense, segments = pl.pallas_call(
        functools.partial(step_kernel, n_tile, n_lev),
        out_shape=(
            jax.ShapeDtypeStruct((tags * width * depth, LANES), F32),
            jax.ShapeDtypeStruct((tags, elements), F32),
            jax.ShapeDtypeStruct((tags, 8), F32),
        ),
        in_specs=[vmem] * 8 + [smem],
        out_specs=(vmem, vmem, vmem),
        scratch_shapes=[
            pltpu.VMEM((4, width + 2, depth + 2, tags, LANES), F32),
            pltpu.VMEM((width, depth, tags, LANES), F32),
            pltpu.VMEM((6, width, depth, LANES), F32),
            pltpu.VMEM((width, depth, LANES), F32),
            pltpu.VMEM((2, 32, LANES), F32),
            pltpu.VMEM((2, 3, depth, LANES), F32),
            pltpu.VMEM((2, 2, depth, LANES), F32),
            pltpu.VMEM((2, 8, LANES), F32),
            pltpu.VMEM((2, 8, LANES), F32),
            pltpu.VMEM((elements // LANES * n_tile, LANES), BF16),
            pltpu.VMEM((elements // LANES * n_tile, 2 * LANES), F32),
            pltpu.VMEM((half * 18, elements), BF16),
            pltpu.VMEM((256, elements), BF16),
            pltpu.VMEM((n_tile, tags + 2, LANES), F32),
            pltpu.VMEM((n_tile, tags + 2, LANES), F32),
            pltpu.VMEM((512, group * LANES), BF16),
            pltpu.VMEM((256, n_tile * LANES), BF16),
            pltpu.VMEM((n_tile, LANES), I32),
            pltpu.VMEM((elements // LANES, LANES), I32),
            pltpu.VMEM((512, 256), F32),
            pltpu.VMEM((256, 512), BF16),
            pltpu.VMEM((n_tile, tags + 1, LANES), F32),
            pltpu.VMEM((n_tile, tags + 1, LANES), F32),
            pltpu.VMEM((half * 8, 512), BF16),
            pltpu.VMEM((2, n_lev, 8, LANES), F32),
            dma,
            dma((n_tile,)),
            dma,
            dma((n_tile,)),
            dma((4,)),
            dma((4,)),
            dma((3, 4)),
            dma((3, 4)),
            dma((n_lev,)),
            dma((n_lev,)),
            pltpu.SemaphoreType.REGULAR,
        ],
        compiler_params=pltpu.CompilerParams(
            collective_id=0, has_side_effects=True, vmem_limit_bytes=56 << 20
        ),
        name="adjoint_step",
    )(
        adjoint.reshape(tags * width * depth, LANES),
        courant,
        diffusion,
        heights,
        dep_coef,
        elem_dest.reshape(elements // LANES, LANES),
        elem_cell.reshape(elements // LANES, LANES),
        seg_map,
        emis_profile,
    )
    return old.reshape(adjoint.shape), sense, segments


def solution(mesh):
    placed = (
        P(None, "tile", "lev", None),
        P(None, "tile", "lev", None),
        P("tile", "lev", None),
        P("tile", None),
        P(None, ("tile", "lev")),
        P(("tile", "lev"), None),
        P(("tile", "lev")),
        P("tile", None),
        P("lev"),
    )
    return jax.shard_map(
        functools.partial(local, mesh.shape["tile"], mesh.shape["lev"]),
        mesh=mesh,
        in_specs=placed,
        out_specs=(
            P(None, "tile", "lev", None),
            P(None, ("tile", "lev")),
            P(None, ("tile", "lev")),
        ),
        check_vma=False,
    )
```

```python
import functools

import jax
import jax.numpy as jnp
from jax import lax
from jax.experimental import pallas as pl
from jax.experimental.pallas import tpu as pltpu
from jax.sharding import PartitionSpec as P

MESH = pl.DeviceIdType.MESH
LANES = 128
F32 = jnp.float32
BF16 = jnp.bfloat16
I32 = jnp.int32
HIGHEST = lax.Precision.HIGHEST


def split2(values):
    first = values.astype(BF16)
    return first, (values - first.astype(F32)).astype(BF16)


def iota(shape, dim):
    return lax.broadcasted_iota(I32, shape, dim)


def rows_to(row, count):
    return jnp.broadcast_to(row, (count, row.shape[-1]))


def nt_dot(a, b, precision=None):
    return lax.dot_general(
        a, b, (((1,), (1,)), ((), ())), precision=precision, preferred_element_type=F32
    )


def one_hot_256(row_int):
    local = rows_to(row_int, 16) - iota((16, row_int.shape[-1]), 0)
    local = local.astype(F32).astype(BF16)
    one, zero = jnp.ones((), BF16), jnp.zeros((), BF16)
    return [jnp.where(local == jnp.full((), 16 * j, BF16), one, zero) for j in range(16)]


EDGE_HI = 18
HI_CELLS = (
    [(0, z) for z in range(16)] + [(1, 0), (1, 15)] + [(1, z) for z in range(1, 15)]
)


def hi_lo(x, z):
    middle = int(x in (1, 2))
    return HI_CELLS.index((middle, z)), x // 2


def step_kernel(
    n_tile,
    n_lev,
    adj,
    cour,
    diff,
    hts,
    coef,
    dest,
    cell,
    seg,
    emis,
    old_out,
    sense_out,
    seg_out,
    state,
    dep,
    weights,
    wet_s,
    zpad,
    fx_r,
    fx_l,
    fz_u,
    fz_d,
    one_d,
    pref,
    pack_a,
    pack_b,
    snd,
    rcv,
    dep_a,
    dep_i,
    cell_b,
    cell_hi,
    dest_hi,
    acc,
    look,
    snd2,
    rcv2,
    look2,
    segs,
    s_a2a,
    r_a2a,
    s_back,
    r_back,
    s_flow,
    r_flow,
    s_halo,
    r_halo,
    s_row,
    r_row,
    second_round,
):
    me = lax.axis_index("tile")
    lev = lax.axis_index("lev")
    right, left = lax.rem(me + 1, n_tile), lax.rem(me + n_tile - 1, n_tile)
    above, below = lax.rem(lev + 1, n_lev), lax.rem(lev + n_lev - 1, n_lev)
    tags, elements = coef.shape
    chunks = elements // LANES
    half = n_tile // 2
    part = half
    depth = 16
    width = 4

    count_z = min(8, n_tile)
    count_y = n_tile // count_z
    my_y, my_z = me // count_z, lax.rem(me, count_z)
    barrier = pltpu.get_barrier_semaphore()

    def signal(semaphore, tile, level):
        pl.semaphore_signal(semaphore, inc=1, device_id=(tile, level), device_id_type=MESH)

    for j in range(1, count_z):
        signal(barrier, my_y * count_z + lax.rem(my_z + j, count_z), lev)
    for j in range(1, count_y):
        signal(barrier, lax.rem(my_y + j, count_y) * count_z + my_z, lev)
    for j in range(1, n_lev):
        signal(barrier, me, lax.rem(lev + j, n_lev))

    def mark(c, carry):
        k_row = (dest[pl.ds(c, 1), :] - me + n_tile) & (n_tile - 1)
        one_d[pl.ds(pl.multiple_of(c * n_tile, n_tile), n_tile), :] = (
            (rows_to(k_row, n_tile) == iota((n_tile, LANES), 0)).astype(F32).astype(BF16)
        )
        return carry

    lax.fori_loop(0, chunks, mark, 0)
    upper = (iota((LANES, 2 * LANES), 0) < iota((LANES, 2 * LANES), 1)).astype(F32).astype(BF16)
    pref[...] = jnp.dot(one_d[...], upper, preferred_element_type=F32)

    sub_half = iota((16, LANES), 0) // 8

    def place(c, before):
        at = pl.ds(pl.multiple_of(c * LANES, LANES), LANES)
        k_row = (dest[pl.ds(c, 1), :] - me + n_tile) & (n_tile - 1)
        block = pl.ds(pl.multiple_of(c * n_tile, n_tile), n_tile)
        mine = rows_to(k_row, n_tile) == iota((n_tile, LANES), 0)
        place_row = jnp.sum(
            jnp.where(mine, pref[block, 0:LANES] + before, 0.0), axis=0, keepdims=True
        ).astype(I32)
        hi_row = k_row & (half - 1)
        lo_row = (k_row // half) * LANES + place_row
        dest_hi[pl.ds(c, 1), :] = hi_row
        for j, piece in enumerate(one_hot_256(lo_row)):
            pack_b[16 * j : 16 * j + 16, at] = piece
        first, second = split2(coef[:, at])
        first = jnp.concatenate([first, first], axis=0)
        second = jnp.concatenate([second, second], axis=0)
        local = (rows_to(hi_row, 16) - sub_half).astype(F32).astype(BF16)
        zero = jnp.zeros((), BF16)
        for j in range(half // 2):
            chosen = local == jnp.full((), 2 * j, BF16)
            row = j // (part // 2) * part * 18 + j % (part // 2) * 16
            pack_a[row : row + 16, at] = jnp.where(chosen, first, zero)
            pack_a[row + part * 8 : row + part * 8 + 16, at] = jnp.where(chosen, second, zero)
        id_row = cell[pl.ds(c, 1), :].astype(F32)
        id_all = jnp.where(
            rows_to(hi_row, half) == iota((half, LANES), 0), rows_to(id_row, half), 0.0
        )
        id_first, id_second = split2(id_all)
        for q in range(half // part):
            row, own = q * part * 18 + part * 16, slice(q * part, q * part + part)
            pack_a[row : row + part, at] = id_first[own]
            pack_a[row + part : row + 2 * part, at] = id_second[own]
        return before + pref[block, LANES : 2 * LANES]

    lax.fori_loop(0, chunks, place, jnp.zeros((n_tile, LANES), F32))
    pl.semaphore_wait(barrier, count_z - 1 + count_y - 1 + n_lev - 1)
    for j in range(1, count_y):
        signal(second_round, lax.rem(my_y + j, count_y) * count_z + my_z, lev)

    seg_row = seg[0:1, :].astype(F32)

    def forward(k):
        return pltpu.make_async_remote_copy(
            src_ref=snd.at[k],
            dst_ref=rcv.at[k],
            send_sem=s_a2a,
            recv_sem=r_a2a.at[k],
            device_id=(lax.rem(me + k, n_tile), lev),
            device_id_type=MESH,
        )

    def back(k):
        return pltpu.make_async_remote_copy(
            src_ref=snd2.at[k],
            dst_ref=rcv2.at[k],
            send_sem=s_back,
            recv_sem=r_back.at[k],
            device_id=(lax.rem(me + n_tile - k, n_tile), lev),
            device_id_type=MESH,
        )

    for q in range(half // part):
        packed = nt_dot(pack_a[q * part * 18 : (q + 1) * part * 18, :], pack_b[...])
        if q == 0 and count_y > 1:
            pl.semaphore_wait(second_round, count_y - 1)
        for i in range(part):
            for d in range(2):
                k, lo = d * half + q * part + i, slice(d * LANES, (d + 1) * LANES)
                at_id = part * 16 + i
                snd[k, 0:tags, :] = (
                    packed[i * 8 : i * 8 + 8, lo]
                    + packed[part * 8 + i * 8 : part * 8 + i * 8 + 8, lo]
                )
                snd[k, tags : tags + 1, :] = (
                    packed[at_id : at_id + 1, lo] + packed[at_id + part : at_id + part + 1, lo]
                )
                snd[k, tags + 1 : tags + 2, :] = seg_row
                if k > 0:
                    forward(k).start()
                else:
                    rcv[0] = snd[0]

    def reorder(z, carry):
        for x in range(width):
            state[0, x + 1, z + 1] = adj[pl.ds(x * depth + z, tags, stride=width * depth), :]
        return carry

    lax.fori_loop(0, depth, reorder, 0)

    levels = iota((depth, LANES), 0) + lev * depth
    for x in range(width):
        wet_s[x] = (levels >= rows_to(hts[x : x + 1, :], depth)).astype(F32)
    fx_r[0, 0] = wet_s[width - 1]
    fx_r[0, 1] = diff[width - 1]
    fx_r[0, 2] = cour[0, width - 1]
    fx_l[0, 0] = wet_s[0]
    fx_l[0, 1] = diff[0]
    for x in range(width):
        fz_u[0, x : x + 1] = diff[x, depth - 1 : depth, :]
        fz_u[0, width + x : width + x + 1] = cour[2, x, depth - 1 : depth, :]
        fz_d[0, x : x + 1] = diff[x, 0:1, :]
        fz_d[0, width + x : width + x + 1] = cour[2, x, 0:1, :]

    def halos(step):
        return [
            pltpu.make_async_remote_copy(
                src_ref=source,
                dst_ref=target,
                send_sem=s_halo.at[step, i],
                recv_sem=r_halo.at[step, i],
                device_id=device,
                device_id_type=MESH,
            )
            for i, (source, target, device) in enumerate(
                (
                    (
                        state.at[step, width, pl.ds(1, depth)],
                        state.at[step, 0, pl.ds(1, depth)],
                        (right, lev),
                    ),
                    (
                        state.at[step, 1, pl.ds(1, depth)],
                        state.at[step, width + 1, pl.ds(1, depth)],
                        (left, lev),
                    ),
                    (
                        state.at[step, pl.ds(1, width), depth],
                        state.at[step, pl.ds(1, width), 0],
                        (me, above),
                    ),
                    (
                        state.at[step, pl.ds(1, width), 1],
                        state.at[step, pl.ds(1, width), depth + 1],
                        (me, below),
                    ),
                )
            )
        ]

    flows = [
        pltpu.make_async_remote_copy(
            src_ref=ref.at[0],
            dst_ref=ref.at[1],
            send_sem=s_flow.at[i],
            recv_sem=r_flow.at[i],
            device_id=device,
            device_id_type=MESH,
        )
        for i, (ref, device) in enumerate(
            ((fx_r, (right, lev)), (fx_l, (left, lev)), (fz_u, (me, above)), (fz_d, (me, below)))
        )
    ]
    for copy in flows:
        copy.start()
    for copy in halos(0):
        copy.start()

    for copy in flows:
        copy.wait_recv()
    inner_left = (me > 0).astype(F32)
    inner_right = (me < n_tile - 1).astype(F32)
    wet_p = [fx_r[1, 0] * inner_left] + [wet_s[x] for x in range(width)] + [fx_l[1, 0] * inner_right]
    diff_p = [fx_r[1, 1]] + [diff[x] for x in range(width)] + [fx_l[1, 1]]
    cour_p = [fx_r[1, 2]] + [cour[0, x] for x in range(width)]

    def face(wet_a, wet_b, diff_a, diff_b, courant):
        opened = wet_a * wet_b
        a = courant * opened
        k = 0.5 * (diff_a + diff_b) * opened
        return jnp.maximum(a, 0.0) + k, k - jnp.minimum(a, 0.0)

    for f in range(width + 1):
        ahead, behind = face(wet_p[f], wet_p[f + 1], diff_p[f], diff_p[f + 1], cour_p[f])
        if f > 0:
            weights[0, f - 1] = ahead
        if f < width:
            weights[1, f] = behind
    last_lane = iota((depth, LANES), 1) == LANES - 1
    for x in range(width):
        zpad[0, 8 : 8 + depth] = diff[x]
        zpad[0, 7:8] = fz_u[1, x : x + 1]
        zpad[0, 8 + depth : 9 + depth] = fz_d[1, x : x + 1]
        zpad[1, 8 : 8 + depth] = cour[2, x]
        zpad[1, 7:8] = fz_u[1, width + x : width + x + 1]
        height = rows_to(hts[x : x + 1, :], depth)
        wet = wet_s[x]
        wet_up = ((levels + 1 >= height) & (levels + 1 < n_lev * depth)).astype(F32)
        wet_dn = ((levels - 1 >= height) & (levels >= 1)).astype(F32)
        ahead, _ = face(wet, wet_up, diff[x], zpad[0, 9 : 9 + depth], cour[2, x])
        _, behind = face(wet_dn, wet, zpad[0, 7 : 7 + depth], diff[x], zpad[1, 7 : 7 + depth])
        weights[2, x] = ahead
        weights[3, x] = behind
        wet_next = jnp.where(last_lane, 0.0, pltpu.roll(wet, LANES - 1, 1))
        ahead, behind = face(wet, wet_next, diff[x], pltpu.roll(diff[x], LANES - 1, 1), cour[1, x])
        weights[4, x] = ahead
        weights[5, x] = pltpu.roll(behind, 1, 1)

    def slot(place_at):
        source = lax.rem(place_at, count_y) * count_z + place_at // count_y
        return lax.rem(me - source + n_tile, n_tile)

    group = dep_a.shape[1] // LANES
    edge_rows, inner_rows = dep_a.shape[0] // 2, dep_i.shape[0] // 2
    acc[...] = jnp.zeros_like(acc)

    def gather_group(g, carry):
        for i in range(group):
            place_at = g * group + i
            k = slot(place_at)

            @pl.when(k > 0)
            def _():
                forward(k).wait_recv()

            at = pl.ds(pl.multiple_of(place_at * LANES, LANES), LANES)
            id_row = rcv[k, tags : tags + 1, :].astype(I32)
            z_row = (id_row >> 7) & 15
            x_row = id_row >> 11
            middle = jnp.where(z_row == 0, 16, jnp.where(z_row == 15, 17, z_row + 17))
            hi_row = jnp.where((x_row == 1) | (x_row == 2), middle, z_row)
            lo_row = (x_row >> 1) * LANES + (id_row & 127)
            cell_hi[pl.ds(place_at, 1), :] = hi_row
            for j, piece in enumerate(one_hot_256(lo_row)):
                cell_b[16 * j : 16 * j + 16, at] = piece
            first, second = split2(rcv[k, 0:tags, :])
            first = jnp.concatenate([first, first], axis=0)
            second = jnp.concatenate([second, second], axis=0)
            local = (rows_to(hi_row, 16) - sub_half).astype(F32).astype(BF16)
            zero = jnp.zeros((), BF16)
            here = slice(i * LANES, (i + 1) * LANES)
            for j in range(16):
                chosen = local == jnp.full((), 2 * j, BF16)
                first_j = jnp.where(chosen, first, zero)
                second_j = jnp.where(chosen, second, zero)
                if j < EDGE_HI // 2:
                    dep_a[16 * j : 16 * j + 16, here] = first_j
                    dep_a[edge_rows + 16 * j : edge_rows + 16 * j + 16, here] = second_j
                else:
                    row = 16 * j - edge_rows
                    dep_i[row : row + 16, at] = first_j
                    dep_i[inner_rows + row : inner_rows + row + 16, at] = second_j
        span = pl.ds(pl.multiple_of(g * group * LANES, group * LANES), group * LANES)
        acc[...] += nt_dot(dep_a[...], cell_b[:, span])
        return carry

    lax.fori_loop(0, n_tile // group, gather_group, 0)

    def deposit_of(which, total, rows):
        for x, z in which:
            hi, lo = hi_lo(x, z)
            row, lo = hi * 8 % edge_rows, slice(lo * LANES, lo * LANES + LANES)
            both = total[row : row + 8, lo] + total[row + rows : row + rows + 8, lo]
            dep[x, z] = both * rows_to(wet_s[x, z : z + 1, :], 8)

    def deposit_inner():
        total = jnp.zeros((2 * inner_rows, 256), F32)
        width_k = min(2048, n_tile * LANES)
        for c in range(n_tile * LANES // width_k):
            span = slice(c * width_k, (c + 1) * width_k)
            total += nt_dot(dep_i[:, span], cell_b[:, span])
        return total

    cells = [(x, z) for x in range(width) for z in range(depth)]
    edge = [c for c in cells if c[0] in (0, width - 1) or c[1] in (0, depth - 1)]
    inner = [c for c in cells if c not in edge]
    deposit_of(edge, acc[...], edge_rows)

    def stage(step, which, sums):
        for x, z in which:

            def weight(d):
                return rows_to(weights[d, x, z : z + 1, :], 8)

            centre = state[step, x + 1, z + 1]
            total = weight(0) * (state[step, x + 2, z + 1] - centre)
            total += weight(1) * (state[step, x, z + 1] - centre)
            total += weight(2) * (state[step, x + 1, z + 2] - centre)
            total += weight(3) * (state[step, x + 1, z] - centre)
            total += weight(4) * (pltpu.roll(centre, LANES - 1, 1) - centre)
            total += weight(5) * (pltpu.roll(centre, 1, 1) - centre)
            total -= dep[x, z] * centre
            new = state[0, x + 1, z + 1] + total * (1.0 / 3.0, 0.5, 1.0)[step]
            state[step + 1, x + 1, z + 1] = new
            if step == 2:
                old_out[pl.ds(x * depth + z, tags, stride=width * depth), :] = new
                sums = sums + new * rows_to(wet_s[x, z : z + 1, :] * emis[z], 8)
        return sums

    def drain(source, target, semaphore):
        pltpu.make_async_remote_copy(
            src_ref=source.at[pl.ds(1, n_tile - 1)],
            dst_ref=target.at[pl.ds(1, n_tile - 1)],
            send_sem=semaphore,
            recv_sem=semaphore,
            device_id=(right, lev),
            device_id_type=MESH,
        ).wait_send()

    sums = jnp.zeros((tags, LANES), F32)
    for copy in halos(0):
        copy.wait_recv()
    stage(0, edge, sums)
    for copy in halos(1):
        copy.start()
    deposit_of(inner, deposit_inner(), inner_rows)
    stage(0, inner, sums)
    stage(1, inner, sums)
    drain(snd, rcv, s_a2a)
    for copy in flows + halos(0):
        copy.wait_send()
    for copy in halos(1):
        copy.wait_recv()
    stage(1, edge, sums)
    for copy in halos(2):
        copy.start()
    sums = stage(2, inner, sums)
    for copy in halos(2):
        copy.wait_recv()
    sums = stage(2, edge, sums)

    same_patch = (iota((LANES, LANES), 0) // 8 == iota((LANES, LANES), 1) // 8).astype(F32)
    patch = jnp.dot(sums, same_patch, precision=HIGHEST, preferred_element_type=F32)
    own_lane = iota((tags, LANES), 1) % 8 == iota((tags, LANES), 0)
    own_row = jnp.sum(jnp.where(own_lane, patch, 0.0), axis=0, keepdims=True)
    for pair in range(16):
        for lo in range(2):
            found = []
            for middle, z in HI_CELLS[2 * pair : 2 * pair + 2]:
                x = ((0, 3), (1, 2))[middle][lo]
                found.append(state[3, x + 1, z + 1])
            first, second = split2(jnp.concatenate(found, axis=0))
            look[16 * pair : 16 * pair + 16, lo * LANES : (lo + 1) * LANES] = first
            look[16 * pair : 16 * pair + 16, 256 + lo * LANES : 256 + (lo + 1) * LANES] = second

    span_blocks = min(8, chunks)

    def read_group(g, carry):
        at = pl.ds(pl.multiple_of(g * span_blocks * LANES, span_blocks * LANES), span_blocks * LANES)
        hot = cell_b[:, at]
        found = jnp.dot(
            look[...], jnp.concatenate([hot, hot], axis=0), preferred_element_type=F32
        )
        for i in range(span_blocks):
            place_at = g * span_blocks + i
            k = slot(place_at)
            hi_all = rows_to(cell_hi[pl.ds(place_at, 1), :], 8)
            value = jnp.zeros((8, LANES), F32)
            for hi in range(32):
                value += jnp.where(
                    hi_all == hi, found[hi * 8 : hi * 8 + 8, i * LANES : (i + 1) * LANES], 0.0
                )
            snd2[k, 0:tags, :] = value
            snd2[k, tags : tags + 1, :] = own_row

            @pl.when(k > 0)
            def _():
                back(k).start()

        return carry

    lax.fori_loop(0, n_tile // span_blocks, read_group, 0)
    rcv2[0] = snd2[0]

    def arrive(k, carry):
        back(k).wait_recv()
        return carry

    lax.fori_loop(1, n_tile, arrive, 0)

    def wanted(j):
        first_segment = (me * n_lev + lax.rem(lev + j, n_lev)) * 8
        return (iota((8, LANES), 0) + first_segment).astype(F32)

    def segment_copy(j):
        return pltpu.make_async_remote_copy(
            src_ref=segs.at[0, j],
            dst_ref=segs.at[1, j],
            send_sem=s_row.at[j],
            recv_sem=r_row.at[j],
            device_id=(me, lax.rem(lev + j, n_lev)),
            device_id_type=MESH,
        )

    wanted_all = [wanted(j) for j in range(n_lev)]

    def add_tile(k, totals):
        named = rows_to(rcv[lax.rem(n_tile - k, n_tile), tags + 1 : tags + 2, :], 8)
        values = rows_to(rcv2[k, tags : tags + 1, :], 8)
        return tuple(
            total + jnp.where(named == want, values, 0.0)
            for total, want in zip(totals, wanted_all)
        )

    by_segment = lax.fori_loop(
        0, n_tile, add_tile, (jnp.zeros((8, LANES), F32),) * n_lev, unroll=4
    )
    for j in range(1, n_lev):
        segs[0, j] = by_segment[j]
        segment_copy(j).start()

    for j in range(half // 2):
        for d in range(2):
            values = jnp.concatenate(
                [rcv2[d * half + 2 * j, 0:tags, :], rcv2[d * half + 2 * j + 1, 0:tags, :]], axis=0
            )
            first, second = split2(values)
            look2[16 * j : 16 * j + 16, d * LANES : (d + 1) * LANES] = first
            look2[16 * j : 16 * j + 16, 256 + d * LANES : 256 + (d + 1) * LANES] = second

    def sense_group(g, carry):
        at = pl.ds(pl.multiple_of(g * span_blocks * LANES, span_blocks * LANES), span_blocks * LANES)
        hot = pack_b[:, at]
        found = jnp.dot(
            look2[...], jnp.concatenate([hot, hot], axis=0), preferred_element_type=F32
        )
        for i in range(span_blocks):
            c = g * span_blocks + i
            one = pl.ds(pl.multiple_of(c * LANES, LANES), LANES)
            hi_all = rows_to(dest_hi[pl.ds(c, 1), :], 8)
            value = jnp.zeros((8, LANES), F32)
            for hi in range(half):
                value += jnp.where(
                    hi_all == hi, found[hi * 8 : hi * 8 + 8, i * LANES : (i + 1) * LANES], 0.0
                )
            sense_out[:, one] = value * coef[:, one]
        return carry

    lax.fori_loop(0, chunks // span_blocks, sense_group, 0)

    drain(snd2, rcv2, s_back)
    for copy in halos(1) + halos(2):
        copy.wait_send()

    total = by_segment[0]
    for j in range(1, n_lev):
        segment_copy(j).wait()
        total = total + segs[1, j]
    seg_out[...] = nt_dot(own_lane.astype(F32), total, precision=HIGHEST)


def write_kernel(old, sense, segments, old_out, sense_out, segments_out, sems):
    pieces = 4
    copies = []
    for i in range(pieces):
        for ref, out in ((old, old_out), (sense, sense_out)):
            if ref is old:
                rows = ref.shape[0] // pieces
                at = (pl.ds(i * rows, rows),)
            else:
                lanes = ref.shape[1] // pieces
                at = (slice(None), pl.ds(i * lanes, lanes))
            copies.append(
                pltpu.make_async_copy(ref.at[at], out.at[at], sems.at[len(copies)])
            )
    copies.append(pltpu.make_async_copy(segments, segments_out, sems.at[len(copies)]))
    for copy in copies:
        copy.start()
    for copy in copies:
        copy.wait()


def local(
    n_tile, n_lev, adjoint, courant, diffusion, heights, dep_coef, elem_dest, elem_cell, seg_map, emis_profile
):
    tags, width, depth, _ = adjoint.shape
    elements = dep_coef.shape[1]
    half = n_tile // 2
    vmem = pl.BlockSpec(memory_space=pltpu.VMEM)
    smem = pl.BlockSpec(memory_space=pltpu.SMEM)
    dma = pltpu.SemaphoreType.DMA
    group = min(32, n_tile)
    old, sense, segments = pl.pallas_call(
        functools.partial(step_kernel, n_tile, n_lev),
        out_shape=(
            jax.ShapeDtypeStruct((tags * width * depth, LANES), F32),
            jax.ShapeDtypeStruct((tags, elements), F32),
            jax.ShapeDtypeStruct((tags, 8), F32),
        ),
        in_specs=[vmem] * 8 + [smem],
        out_specs=(vmem, vmem, vmem),
        scratch_shapes=[
            pltpu.VMEM((4, width + 2, depth + 2, tags, LANES), F32),
            pltpu.VMEM((width, depth, tags, LANES), F32),
            pltpu.VMEM((6, width, depth, LANES), F32),
            pltpu.VMEM((width, depth, LANES), F32),
            pltpu.VMEM((2, 32, LANES), F32),
            pltpu.VMEM((2, 3, depth, LANES), F32),
            pltpu.VMEM((2, 2, depth, LANES), F32),
            pltpu.VMEM((2, 8, LANES), F32),
            pltpu.VMEM((2, 8, LANES), F32),
            pltpu.VMEM((elements // LANES * n_tile, LANES), BF16),
            pltpu.VMEM((elements // LANES * n_tile, 2 * LANES), F32),
            pltpu.VMEM((half * 18, elements), BF16),
            pltpu.VMEM((256, elements), BF16),
            pltpu.VMEM((n_tile, tags + 2, LANES), F32),
            pltpu.VMEM((n_tile, tags + 2, LANES), F32),
            pltpu.VMEM((16 * EDGE_HI, group * LANES), BF16),
            pltpu.VMEM((512 - 16 * EDGE_HI, n_tile * LANES), BF16),
            pltpu.VMEM((256, n_tile * LANES), BF16),
            pltpu.VMEM((n_tile, LANES), I32),
            pltpu.VMEM((elements // LANES, LANES), I32),
            pltpu.VMEM((16 * EDGE_HI, 256), F32),
            pltpu.VMEM((256, 512), BF16),
            pltpu.VMEM((n_tile, tags + 1, LANES), F32),
            pltpu.VMEM((n_tile, tags + 1, LANES), F32),
            pltpu.VMEM((half * 8, 512), BF16),
            pltpu.VMEM((2, n_lev, 8, LANES), F32),
            dma,
            dma((n_tile,)),
            dma,
            dma((n_tile,)),
            dma((4,)),
            dma((4,)),
            dma((3, 4)),
            dma((3, 4)),
            dma((n_lev,)),
            dma((n_lev,)),
            pltpu.SemaphoreType.REGULAR,
        ],
        compiler_params=pltpu.CompilerParams(
            collective_id=0, has_side_effects=True, vmem_limit_bytes=56 << 20
        ),
        name="adjoint_step",
    )(
        adjoint.reshape(tags * width * depth, LANES),
        courant,
        diffusion,
        heights,
        dep_coef,
        elem_dest.reshape(elements // LANES, LANES),
        elem_cell.reshape(elements // LANES, LANES),
        seg_map,
        emis_profile,
    )
    anywhere = pl.BlockSpec(memory_space=pl.ANY)
    results = (old, sense, segments)
    old, sense, segments = pl.pallas_call(
        write_kernel,
        out_shape=tuple(jax.ShapeDtypeStruct(r.shape, r.dtype) for r in results),
        in_specs=[vmem] * 3,
        out_specs=(anywhere,) * 3,
        scratch_shapes=[dma((9,))],
        name="write_results",
    )(*results)
    return old.reshape(adjoint.shape), sense, segments


def solution(mesh):
    placed = (
        P(None, "tile", "lev", None),
        P(None, "tile", "lev", None),
        P("tile", "lev", None),
        P("tile", None),
        P(None, ("tile", "lev")),
        P(("tile", "lev"), None),
        P(("tile", "lev")),
        P("tile", None),
        P("lev"),
    )
    return jax.shard_map(
        functools.partial(local, mesh.shape["tile"], mesh.shape["lev"]),
        mesh=mesh,
        in_specs=placed,
        out_specs=(
            P(None, "tile", "lev", None),
            P(None, ("tile", "lev")),
            P(None, ("tile", "lev")),
        ),
        check_vma=False,
    )
```

```python
import functools

import jax
import jax.numpy as jnp
from jax import lax
from jax.experimental import pallas as pl
from jax.experimental.pallas import tpu as pltpu
from jax.sharding import PartitionSpec as P

MESH = pl.DeviceIdType.MESH
LANES = 128
F32 = jnp.float32
BF16 = jnp.bfloat16
I32 = jnp.int32
HIGHEST = lax.Precision.HIGHEST


def split2(values):
    first = values.astype(BF16)
    return first, (values - first.astype(F32)).astype(BF16)


def iota(shape, dim):
    return lax.broadcasted_iota(I32, shape, dim)


def rows_to(row, count):
    return jnp.broadcast_to(row, (count, row.shape[-1]))


def nt_dot(a, b, precision=None):
    return lax.dot_general(
        a, b, (((1,), (1,)), ((), ())), precision=precision, preferred_element_type=F32
    )


def one_hot_256(row_int):
    local = rows_to(row_int, 16) - iota((16, row_int.shape[-1]), 0)
    local = local.astype(F32).astype(BF16)
    one, zero = jnp.ones((), BF16), jnp.zeros((), BF16)
    return [jnp.where(local == jnp.full((), 16 * j, BF16), one, zero) for j in range(16)]


EDGE_HI = 18
HI_CELLS = (
    [(0, z) for z in range(16)] + [(1, 0), (1, 15)] + [(1, z) for z in range(1, 15)]
)


def hi_lo(x, z):
    middle = int(x in (1, 2))
    return HI_CELLS.index((middle, z)), x // 2


def step_kernel(
    n_tile,
    n_lev,
    adj,
    cour,
    diff,
    hts,
    coef,
    dest,
    cell,
    seg,
    emis,
    old_out,
    sense_out,
    seg_out,
    state,
    dep,
    weights,
    wet_s,
    zpad,
    fx_r,
    fx_l,
    fz_u,
    fz_d,
    one_d,
    pref,
    pack_a,
    pack_b,
    snd,
    rcv,
    dep_a,
    dep_i,
    cell_b,
    cell_hi,
    dest_hi,
    acc,
    look,
    inside,
    snd2,
    rcv2,
    look2,
    segs,
    s_a2a,
    r_a2a,
    s_back,
    r_back,
    s_flow,
    r_flow,
    s_halo,
    r_halo,
    s_row,
    r_row,
    second_round,
):
    me = lax.axis_index("tile")
    lev = lax.axis_index("lev")
    right, left = lax.rem(me + 1, n_tile), lax.rem(me + n_tile - 1, n_tile)
    above, below = lax.rem(lev + 1, n_lev), lax.rem(lev + n_lev - 1, n_lev)
    tags, elements = coef.shape
    chunks = elements // LANES
    half = n_tile // 2
    part = half
    depth = 16
    width = 4

    count_z = min(8, n_tile)
    count_y = n_tile // count_z
    my_y, my_z = me // count_z, lax.rem(me, count_z)
    barrier = pltpu.get_barrier_semaphore()

    def signal(semaphore, tile, level):
        pl.semaphore_signal(semaphore, inc=1, device_id=(tile, level), device_id_type=MESH)

    for j in range(1, count_z):
        signal(barrier, my_y * count_z + lax.rem(my_z + j, count_z), lev)
    for j in range(1, count_y):
        signal(barrier, lax.rem(my_y + j, count_y) * count_z + my_z, lev)
    for j in range(1, n_lev):
        signal(barrier, me, lax.rem(lev + j, n_lev))

    def mark(c, carry):
        k_row = (dest[pl.ds(c, 1), :] - me + n_tile) & (n_tile - 1)
        one_d[pl.ds(pl.multiple_of(c * n_tile, n_tile), n_tile), :] = (
            (rows_to(k_row, n_tile) == iota((n_tile, LANES), 0)).astype(F32).astype(BF16)
        )
        return carry

    lax.fori_loop(0, chunks, mark, 0)
    upper = (iota((LANES, 2 * LANES), 0) < iota((LANES, 2 * LANES), 1)).astype(F32).astype(BF16)
    pref[...] = jnp.dot(one_d[...], upper, preferred_element_type=F32)

    sub_half = iota((16, LANES), 0) // 8

    def place(c, before):
        at = pl.ds(pl.multiple_of(c * LANES, LANES), LANES)
        k_row = (dest[pl.ds(c, 1), :] - me + n_tile) & (n_tile - 1)
        block = pl.ds(pl.multiple_of(c * n_tile, n_tile), n_tile)
        mine = rows_to(k_row, n_tile) == iota((n_tile, LANES), 0)
        place_row = jnp.sum(
            jnp.where(mine, pref[block, 0:LANES] + before, 0.0), axis=0, keepdims=True
        ).astype(I32)
        hi_row = k_row & (half - 1)
        lo_row = (k_row // half) * LANES + place_row
        dest_hi[pl.ds(c, 1), :] = hi_row
        for j, piece in enumerate(one_hot_256(lo_row)):
            pack_b[16 * j : 16 * j + 16, at] = piece
        first, second = split2(coef[:, at])
        first = jnp.concatenate([first, first], axis=0)
        second = jnp.concatenate([second, second], axis=0)
        local = (rows_to(hi_row, 16) - sub_half).astype(F32).astype(BF16)
        zero = jnp.zeros((), BF16)
        for j in range(half // 2):
            chosen = local == jnp.full((), 2 * j, BF16)
            row = j // (part // 2) * part * 18 + j % (part // 2) * 16
            pack_a[row : row + 16, at] = jnp.where(chosen, first, zero)
            pack_a[row + part * 8 : row + part * 8 + 16, at] = jnp.where(chosen, second, zero)
        id_row = cell[pl.ds(c, 1), :].astype(F32)
        id_all = jnp.where(
            rows_to(hi_row, half) == iota((half, LANES), 0), rows_to(id_row, half), 0.0
        )
        id_first, id_second = split2(id_all)
        for q in range(half // part):
            row, own = q * part * 18 + part * 16, slice(q * part, q * part + part)
            pack_a[row : row + part, at] = id_first[own]
            pack_a[row + part : row + 2 * part, at] = id_second[own]
        return before + pref[block, LANES : 2 * LANES]

    lax.fori_loop(0, chunks, place, jnp.zeros((n_tile, LANES), F32))
    pl.semaphore_wait(barrier, count_z - 1 + count_y - 1 + n_lev - 1)
    for j in range(1, count_y):
        signal(second_round, lax.rem(my_y + j, count_y) * count_z + my_z, lev)

    seg_row = seg[0:1, :].astype(F32)

    def forward(k):
        return pltpu.make_async_remote_copy(
            src_ref=snd.at[k],
            dst_ref=rcv.at[k],
            send_sem=s_a2a,
            recv_sem=r_a2a.at[k],
            device_id=(lax.rem(me + k, n_tile), lev),
            device_id_type=MESH,
        )

    def back(k):
        return pltpu.make_async_remote_copy(
            src_ref=snd2.at[k],
            dst_ref=rcv2.at[k],
            send_sem=s_back,
            recv_sem=r_back.at[k],
            device_id=(lax.rem(me + n_tile - k, n_tile), lev),
            device_id_type=MESH,
        )

    for q in range(half // part):
        packed = nt_dot(pack_a[q * part * 18 : (q + 1) * part * 18, :], pack_b[...])
        if q == 0 and count_y > 1:
            pl.semaphore_wait(second_round, count_y - 1)
        for i in range(part):
            for d in range(2):
                k, lo = d * half + q * part + i, slice(d * LANES, (d + 1) * LANES)
                at_id = part * 16 + i
                snd[k, 0:tags, :] = (
                    packed[i * 8 : i * 8 + 8, lo]
                    + packed[part * 8 + i * 8 : part * 8 + i * 8 + 8, lo]
                )
                snd[k, tags : tags + 1, :] = (
                    packed[at_id : at_id + 1, lo] + packed[at_id + part : at_id + part + 1, lo]
                )
                snd[k, tags + 1 : tags + 2, :] = seg_row
                if k > 0:
                    forward(k).start()
                else:
                    rcv[0] = snd[0]

    def reorder(z, carry):
        for x in range(width):
            state[0, x + 1, z + 1] = adj[pl.ds(x * depth + z, tags, stride=width * depth), :]
        return carry

    lax.fori_loop(0, depth, reorder, 0)

    levels = iota((depth, LANES), 0) + lev * depth
    for x in range(width):
        wet_s[x] = (levels >= rows_to(hts[x : x + 1, :], depth)).astype(F32)
    fx_r[0, 0] = wet_s[width - 1]
    fx_r[0, 1] = diff[width - 1]
    fx_r[0, 2] = cour[0, width - 1]
    fx_l[0, 0] = wet_s[0]
    fx_l[0, 1] = diff[0]
    for x in range(width):
        fz_u[0, x : x + 1] = diff[x, depth - 1 : depth, :]
        fz_u[0, width + x : width + x + 1] = cour[2, x, depth - 1 : depth, :]
        fz_d[0, x : x + 1] = diff[x, 0:1, :]
        fz_d[0, width + x : width + x + 1] = cour[2, x, 0:1, :]

    def halos(step):
        return [
            pltpu.make_async_remote_copy(
                src_ref=source,
                dst_ref=target,
                send_sem=s_halo.at[step, i],
                recv_sem=r_halo.at[step, i],
                device_id=device,
                device_id_type=MESH,
            )
            for i, (source, target, device) in enumerate(
                (
                    (
                        state.at[step, width, pl.ds(1, depth)],
                        state.at[step, 0, pl.ds(1, depth)],
                        (right, lev),
                    ),
                    (
                        state.at[step, 1, pl.ds(1, depth)],
                        state.at[step, width + 1, pl.ds(1, depth)],
                        (left, lev),
                    ),
                    (
                        state.at[step, pl.ds(1, width), depth],
                        state.at[step, pl.ds(1, width), 0],
                        (me, above),
                    ),
                    (
                        state.at[step, pl.ds(1, width), 1],
                        state.at[step, pl.ds(1, width), depth + 1],
                        (me, below),
                    ),
                )
            )
        ]

    flows = [
        pltpu.make_async_remote_copy(
            src_ref=ref.at[0],
            dst_ref=ref.at[1],
            send_sem=s_flow.at[i],
            recv_sem=r_flow.at[i],
            device_id=device,
            device_id_type=MESH,
        )
        for i, (ref, device) in enumerate(
            ((fx_r, (right, lev)), (fx_l, (left, lev)), (fz_u, (me, above)), (fz_d, (me, below)))
        )
    ]
    for copy in flows:
        copy.start()
    for copy in halos(0):
        copy.start()

    for copy in flows:
        copy.wait_recv()
    inner_left = (me > 0).astype(F32)
    inner_right = (me < n_tile - 1).astype(F32)
    wet_p = [fx_r[1, 0] * inner_left] + [wet_s[x] for x in range(width)] + [fx_l[1, 0] * inner_right]
    diff_p = [fx_r[1, 1]] + [diff[x] for x in range(width)] + [fx_l[1, 1]]
    cour_p = [fx_r[1, 2]] + [cour[0, x] for x in range(width)]

    def face(wet_a, wet_b, diff_a, diff_b, courant):
        opened = wet_a * wet_b
        a = courant * opened
        k = 0.5 * (diff_a + diff_b) * opened
        return jnp.maximum(a, 0.0) + k, k - jnp.minimum(a, 0.0)

    for f in range(width + 1):
        ahead, behind = face(wet_p[f], wet_p[f + 1], diff_p[f], diff_p[f + 1], cour_p[f])
        if f > 0:
            weights[0, f - 1] = ahead
        if f < width:
            weights[1, f] = behind
    last_lane = iota((depth, LANES), 1) == LANES - 1
    for x in range(width):
        zpad[0, 8 : 8 + depth] = diff[x]
        zpad[0, 7:8] = fz_u[1, x : x + 1]
        zpad[0, 8 + depth : 9 + depth] = fz_d[1, x : x + 1]
        zpad[1, 8 : 8 + depth] = cour[2, x]
        zpad[1, 7:8] = fz_u[1, width + x : width + x + 1]
        height = rows_to(hts[x : x + 1, :], depth)
        wet = wet_s[x]
        wet_up = ((levels + 1 >= height) & (levels + 1 < n_lev * depth)).astype(F32)
        wet_dn = ((levels - 1 >= height) & (levels >= 1)).astype(F32)
        ahead, _ = face(wet, wet_up, diff[x], zpad[0, 9 : 9 + depth], cour[2, x])
        _, behind = face(wet_dn, wet, zpad[0, 7 : 7 + depth], diff[x], zpad[1, 7 : 7 + depth])
        weights[2, x] = ahead
        weights[3, x] = behind
        wet_next = jnp.where(last_lane, 0.0, pltpu.roll(wet, LANES - 1, 1))
        ahead, behind = face(wet, wet_next, diff[x], pltpu.roll(diff[x], LANES - 1, 1), cour[1, x])
        weights[4, x] = ahead
        weights[5, x] = pltpu.roll(behind, 1, 1)

    def slot(place_at):
        source = lax.rem(place_at, count_y) * count_z + place_at // count_y
        return lax.rem(me - source + n_tile, n_tile)

    group = dep_a.shape[1] // LANES
    edge_rows, inner_rows = dep_a.shape[0] // 2, dep_i.shape[0] // 2
    acc[...] = jnp.zeros_like(acc)

    def gather_group(g, carry):
        for i in range(group):
            place_at = g * group + i
            k = slot(place_at)

            @pl.when(k > 0)
            def _():
                forward(k).wait_recv()

            at = pl.ds(pl.multiple_of(place_at * LANES, LANES), LANES)
            id_row = rcv[k, tags : tags + 1, :].astype(I32)
            z_row = (id_row >> 7) & 15
            x_row = id_row >> 11
            middle = jnp.where(z_row == 0, 16, jnp.where(z_row == 15, 17, z_row + 17))
            hi_row = jnp.where((x_row == 1) | (x_row == 2), middle, z_row)
            lo_row = (x_row >> 1) * LANES + (id_row & 127)
            cell_hi[pl.ds(place_at, 1), :] = hi_row
            for j, piece in enumerate(one_hot_256(lo_row)):
                cell_b[16 * j : 16 * j + 16, at] = piece
            first, second = split2(rcv[k, 0:tags, :])
            first = jnp.concatenate([first, first], axis=0)
            second = jnp.concatenate([second, second], axis=0)
            local = (rows_to(hi_row, 16) - sub_half).astype(F32).astype(BF16)
            zero = jnp.zeros((), BF16)
            here = slice(i * LANES, (i + 1) * LANES)
            for j in range(16):
                chosen = local == jnp.full((), 2 * j, BF16)
                first_j = jnp.where(chosen, first, zero)
                second_j = jnp.where(chosen, second, zero)
                if j < EDGE_HI // 2:
                    dep_a[16 * j : 16 * j + 16, here] = first_j
                    dep_a[edge_rows + 16 * j : edge_rows + 16 * j + 16, here] = second_j
                else:
                    row = 16 * j - edge_rows
                    dep_i[row : row + 16, at] = first_j
                    dep_i[inner_rows + row : inner_rows + row + 16, at] = second_j
        span = pl.ds(pl.multiple_of(g * group * LANES, group * LANES), group * LANES)
        acc[...] += nt_dot(dep_a[...], cell_b[:, span])
        return carry

    lax.fori_loop(0, n_tile // group, gather_group, 0)

    def deposit_of(which, total, rows):
        for x, z in which:
            hi, lo = hi_lo(x, z)
            row, lo = hi * 8 % edge_rows, slice(lo * LANES, lo * LANES + LANES)
            both = total[row : row + 8, lo] + total[row + rows : row + rows + 8, lo]
            dep[x, z] = both * rows_to(wet_s[x, z : z + 1, :], 8)

    def deposit_inner():
        total = jnp.zeros((2 * inner_rows, 256), F32)
        width_k = min(2048, n_tile * LANES)
        for c in range(n_tile * LANES // width_k):
            span = slice(c * width_k, (c + 1) * width_k)
            total += nt_dot(dep_i[:, span], cell_b[:, span])
        return total

    cells = [(x, z) for x in range(width) for z in range(depth)]
    edge = [c for c in cells if c[0] in (0, width - 1) or c[1] in (0, depth - 1)]
    inner = [c for c in cells if c not in edge]
    deposit_of(edge, acc[...], edge_rows)

    def stage(step, which, sums):
        for x, z in which:

            def weight(d):
                return rows_to(weights[d, x, z : z + 1, :], 8)

            centre = state[step, x + 1, z + 1]
            total = weight(0) * (state[step, x + 2, z + 1] - centre)
            total += weight(1) * (state[step, x, z + 1] - centre)
            total += weight(2) * (state[step, x + 1, z + 2] - centre)
            total += weight(3) * (state[step, x + 1, z] - centre)
            total += weight(4) * (pltpu.roll(centre, LANES - 1, 1) - centre)
            total += weight(5) * (pltpu.roll(centre, 1, 1) - centre)
            total -= dep[x, z] * centre
            new = state[0, x + 1, z + 1] + total * (1.0 / 3.0, 0.5, 1.0)[step]
            state[step + 1, x + 1, z + 1] = new
            if step == 2:
                old_out[pl.ds(x * depth + z, tags, stride=width * depth), :] = new
                sums = sums + new * rows_to(wet_s[x, z : z + 1, :] * emis[z], 8)
        return sums

    def drain(source, target, semaphore):
        pltpu.make_async_remote_copy(
            src_ref=source.at[pl.ds(1, n_tile - 1)],
            dst_ref=target.at[pl.ds(1, n_tile - 1)],
            send_sem=semaphore,
            recv_sem=semaphore,
            device_id=(right, lev),
            device_id_type=MESH,
        ).wait_send()

    sums = jnp.zeros((tags, LANES), F32)
    for copy in halos(0):
        copy.wait_recv()
    stage(0, edge, sums)
    for copy in halos(1):
        copy.start()
    deposit_of(inner, deposit_inner(), inner_rows)
    stage(0, inner, sums)
    stage(1, inner, sums)
    drain(snd, rcv, s_a2a)
    for copy in flows + halos(0):
        copy.wait_send()
    for copy in halos(1):
        copy.wait_recv()
    stage(1, edge, sums)
    for copy in halos(2):
        copy.start()
    sums = stage(2, inner, sums)

    def table(pairs):
        for pair in pairs:
            for lo in range(2):
                found = []
                for middle, z in HI_CELLS[2 * pair : 2 * pair + 2]:
                    x = ((0, 3), (1, 2))[middle][lo]
                    found.append(state[3, x + 1, z + 1])
                first, second = split2(jnp.concatenate(found, axis=0))
                at = slice(16 * pair, 16 * pair + 16)
                look[at, lo * LANES : (lo + 1) * LANES] = first
                look[at, 256 + lo * LANES : 256 + (lo + 1) * LANES] = second

    span_blocks = min(8, chunks)
    edge_hi, inner_hi = range(EDGE_HI), range(EDGE_HI, 32)

    def read_span(numbers, final):
        def read_group(g, carry):
            at = pl.ds(
                pl.multiple_of(g * span_blocks * LANES, span_blocks * LANES), span_blocks * LANES
            )
            hot = cell_b[:, at]
            found = jnp.dot(
                look[8 * numbers.start : 8 * numbers.stop, :],
                jnp.concatenate([hot, hot], axis=0),
                preferred_element_type=F32,
            )
            for i in range(span_blocks):
                place_at = g * span_blocks + i
                k = slot(place_at)
                hi_all = rows_to(cell_hi[pl.ds(place_at, 1), :], 8)
                value = inside[place_at] if final else jnp.zeros((8, LANES), F32)
                for n, hi in enumerate(numbers):
                    value += jnp.where(
                        hi_all == hi, found[n * 8 : n * 8 + 8, i * LANES : (i + 1) * LANES], 0.0
                    )
                if not final:
                    inside[place_at] = value
                else:
                    snd2[k, 0:tags, :] = value
                    snd2[k, tags : tags + 1, :] = own_row

                    @pl.when(k > 0)
                    def _():
                        back(k).start()

            return carry

        lax.fori_loop(0, n_tile // span_blocks, read_group, 0)

    table(range(EDGE_HI // 2, 16))
    read_span(inner_hi, False)
    for copy in halos(2):
        copy.wait_recv()
    sums = stage(2, edge, sums)

    same_patch = (iota((LANES, LANES), 0) // 8 == iota((LANES, LANES), 1) // 8).astype(F32)
    patch = jnp.dot(sums, same_patch, precision=HIGHEST, preferred_element_type=F32)
    own_lane = iota((tags, LANES), 1) % 8 == iota((tags, LANES), 0)
    own_row = jnp.sum(jnp.where(own_lane, patch, 0.0), axis=0, keepdims=True)
    table(range(EDGE_HI // 2))
    read_span(edge_hi, True)
    rcv2[0] = snd2[0]

    def arrive(k, carry):
        back(k).wait_recv()
        return carry

    lax.fori_loop(1, n_tile, arrive, 0)

    def wanted(j):
        first_segment = (me * n_lev + lax.rem(lev + j, n_lev)) * 8
        return (iota((8, LANES), 0) + first_segment).astype(F32)

    def segment_copy(j):
        return pltpu.make_async_remote_copy(
            src_ref=segs.at[0, j],
            dst_ref=segs.at[1, j],
            send_sem=s_row.at[j],
            recv_sem=r_row.at[j],
            device_id=(me, lax.rem(lev + j, n_lev)),
            device_id_type=MESH,
        )

    wanted_all = [wanted(j) for j in range(n_lev)]

    def add_tile(k, totals):
        named = rows_to(rcv[lax.rem(n_tile - k, n_tile), tags + 1 : tags + 2, :], 8)
        values = rows_to(rcv2[k, tags : tags + 1, :], 8)
        return tuple(
            total + jnp.where(named == want, values, 0.0)
            for total, want in zip(totals, wanted_all)
        )

    by_segment = lax.fori_loop(
        0, n_tile, add_tile, (jnp.zeros((8, LANES), F32),) * n_lev, unroll=4
    )
    for j in range(1, n_lev):
        segs[0, j] = by_segment[j]
        segment_copy(j).start()

    for j in range(half // 2):
        for d in range(2):
            values = jnp.concatenate(
                [rcv2[d * half + 2 * j, 0:tags, :], rcv2[d * half + 2 * j + 1, 0:tags, :]], axis=0
            )
            first, second = split2(values)
            look2[16 * j : 16 * j + 16, d * LANES : (d + 1) * LANES] = first
            look2[16 * j : 16 * j + 16, 256 + d * LANES : 256 + (d + 1) * LANES] = second

    def sense_group(g, carry):
        at = pl.ds(pl.multiple_of(g * span_blocks * LANES, span_blocks * LANES), span_blocks * LANES)
        hot = pack_b[:, at]
        found = jnp.dot(
            look2[...], jnp.concatenate([hot, hot], axis=0), preferred_element_type=F32
        )
        for i in range(span_blocks):
            c = g * span_blocks + i
            one = pl.ds(pl.multiple_of(c * LANES, LANES), LANES)
            hi_all = rows_to(dest_hi[pl.ds(c, 1), :], 8)
            value = jnp.zeros((8, LANES), F32)
            for hi in range(half):
                value += jnp.where(
                    hi_all == hi, found[hi * 8 : hi * 8 + 8, i * LANES : (i + 1) * LANES], 0.0
                )
            sense_out[:, one] = value * coef[:, one]
        return carry

    lax.fori_loop(0, chunks // span_blocks, sense_group, 0)

    drain(snd2, rcv2, s_back)
    for copy in halos(1) + halos(2):
        copy.wait_send()

    total = by_segment[0]
    for j in range(1, n_lev):
        segment_copy(j).wait()
        total = total + segs[1, j]
    seg_out[...] = nt_dot(own_lane.astype(F32), total, precision=HIGHEST)


def write_kernel(old, sense, segments, old_out, sense_out, segments_out, sems):
    pieces = 1
    copies = []
    for i in range(pieces):
        for ref, out in ((old, old_out), (sense, sense_out)):
            if ref is old:
                rows = ref.shape[0] // pieces
                at = (pl.ds(i * rows, rows),)
            else:
                lanes = ref.shape[1] // pieces
                at = (slice(None), pl.ds(i * lanes, lanes))
            copies.append(
                pltpu.make_async_copy(ref.at[at], out.at[at], sems.at[len(copies)])
            )
    copies.append(pltpu.make_async_copy(segments, segments_out, sems.at[len(copies)]))
    for copy in copies:
        copy.start()
    for copy in copies:
        copy.wait()


def local(
    n_tile, n_lev, adjoint, courant, diffusion, heights, dep_coef, elem_dest, elem_cell, seg_map, emis_profile
):
    tags, width, depth, _ = adjoint.shape
    elements = dep_coef.shape[1]
    half = n_tile // 2
    vmem = pl.BlockSpec(memory_space=pltpu.VMEM)
    smem = pl.BlockSpec(memory_space=pltpu.SMEM)
    dma = pltpu.SemaphoreType.DMA
    group = min(32, n_tile)
    old, sense, segments = pl.pallas_call(
        functools.partial(step_kernel, n_tile, n_lev),
        out_shape=(
            jax.ShapeDtypeStruct((tags * width * depth, LANES), F32),
            jax.ShapeDtypeStruct((tags, elements), F32),
            jax.ShapeDtypeStruct((tags, 8), F32),
        ),
        in_specs=[vmem] * 8 + [smem],
        out_specs=(vmem, vmem, vmem),
        scratch_shapes=[
            pltpu.VMEM((4, width + 2, depth + 2, tags, LANES), F32),
            pltpu.VMEM((width, depth, tags, LANES), F32),
            pltpu.VMEM((6, width, depth, LANES), F32),
            pltpu.VMEM((width, depth, LANES), F32),
            pltpu.VMEM((2, 32, LANES), F32),
            pltpu.VMEM((2, 3, depth, LANES), F32),
            pltpu.VMEM((2, 2, depth, LANES), F32),
            pltpu.VMEM((2, 8, LANES), F32),
            pltpu.VMEM((2, 8, LANES), F32),
            pltpu.VMEM((elements // LANES * n_tile, LANES), BF16),
            pltpu.VMEM((elements // LANES * n_tile, 2 * LANES), F32),
            pltpu.VMEM((half * 18, elements), BF16),
            pltpu.VMEM((256, elements), BF16),
            pltpu.VMEM((n_tile, tags + 2, LANES), F32),
            pltpu.VMEM((n_tile, tags + 2, LANES), F32),
            pltpu.VMEM((16 * EDGE_HI, group * LANES), BF16),
            pltpu.VMEM((512 - 16 * EDGE_HI, n_tile * LANES), BF16),
            pltpu.VMEM((256, n_tile * LANES), BF16),
            pltpu.VMEM((n_tile, LANES), I32),
            pltpu.VMEM((elements // LANES, LANES), I32),
            pltpu.VMEM((16 * EDGE_HI, 256), F32),
            pltpu.VMEM((256, 512), BF16),
            pltpu.VMEM((n_tile, tags, LANES), F32),
            pltpu.VMEM((n_tile, tags + 1, LANES), F32),
            pltpu.VMEM((n_tile, tags + 1, LANES), F32),
            pltpu.VMEM((half * 8, 512), BF16),
            pltpu.VMEM((2, n_lev, 8, LANES), F32),
            dma,
            dma((n_tile,)),
            dma,
            dma((n_tile,)),
            dma((4,)),
            dma((4,)),
            dma((3, 4)),
            dma((3, 4)),
            dma((n_lev,)),
            dma((n_lev,)),
            pltpu.SemaphoreType.REGULAR,
        ],
        compiler_params=pltpu.CompilerParams(
            collective_id=0, has_side_effects=True, vmem_limit_bytes=56 << 20
        ),
        name="adjoint_step",
    )(
        adjoint.reshape(tags * width * depth, LANES),
        courant,
        diffusion,
        heights,
        dep_coef,
        elem_dest.reshape(elements // LANES, LANES),
        elem_cell.reshape(elements // LANES, LANES),
        seg_map,
        emis_profile,
    )
    anywhere = pl.BlockSpec(memory_space=pl.ANY)
    results = (old, sense, segments)
    old, sense, segments = pl.pallas_call(
        write_kernel,
        out_shape=tuple(jax.ShapeDtypeStruct(r.shape, r.dtype) for r in results),
        in_specs=[vmem] * 3,
        out_specs=(anywhere,) * 3,
        scratch_shapes=[dma((9,))],
        name="write_results",
    )(*results)
    return old.reshape(adjoint.shape), sense, segments


def solution(mesh):
    placed = (
        P(None, "tile", "lev", None),
        P(None, "tile", "lev", None),
        P("tile", "lev", None),
        P("tile", None),
        P(None, ("tile", "lev")),
        P(("tile", "lev"), None),
        P(("tile", "lev")),
        P("tile", None),
        P("lev"),
    )
    return jax.shard_map(
        functools.partial(local, mesh.shape["tile"], mesh.shape["lev"]),
        mesh=mesh,
        in_specs=placed,
        out_specs=(
            P(None, "tile", "lev", None),
            P(None, ("tile", "lev")),
            P(None, ("tile", "lev")),
        ),
        check_vma=False,
    )
```
